32 devices in a mesh: groups: 2 (over x), leaf: 16 (over z, y, core).
Axes of the slice: x: 2, y: 2, z: 4, core: 2. Of those that a mesh axis runs over, the one named last changes fastest.
Arguments:
- right_side: float32 [65536, 256], P(('groups', 'leaf')), parts along dimension 0, may hold values from -6 to 6
- cotangent: float32 [65536, 256], P(('groups', 'leaf')), parts along dimension 0, may hold values from -6 to 6
- coeff_basis: float32 [4, 64, 65536], P(None, None, ('groups', 'leaf')), parts along dimension 2, may hold values from -1 to 1
- saved_basis: float32 [4, 64, 65536], P(None, None, ('groups', 'leaf')), parts along dimension 2, may hold values from -0.24 to 0.24
- node_inverse: float32 [30, 128, 128], P('groups'), parts along dimension 0, may hold values from -1 to 2.5
- leaf_rows: int32 [32], P(('groups', 'leaf')), parts along dimension 0, may hold values from 1 to 2048, 24576 in all
Outputs:
- solution: float32 [65536, 256], P(('groups', 'leaf')), parts along dimension 0
- grad_left: bfloat16 [4, 64, 65536], P(None, None, ('groups', 'leaf')), parts along dimension 2
- grad_right: bfloat16 [4, 64, 65536], P(None, None, ('groups', 'leaf')), parts along dimension 2
The draws below stay inside these ranges and needn't reach their ends.
There are 2 independent parts, one for each index of `groups`. The reference program is written for one: setup_inputs(seed, part) draws one part's arguments, and reference() takes and returns one part's arrays. A program takes and returns all parts, laid end to end along the dimension named above; each array names one. Nothing has to cross between parts.
Inputs may be any that keep to these rules, and one draw needn't show every extreme that they name: `leaf_rows`: every leaf has at least one live row; the live rows of all leaves sum to 24576, and some leaf has all 2048 rows live.
All inputs are finite; a program needn't handle non-finite values. No bound on the sum of `leaf_rows` on one device may be relied on, other than what follows from the above.
Results may differ from the reference program's by a relative error of at most 0.001.
Values sent between devices are 32-bit elements; how exact they have to be, the bound alone decides.
A program may use at most 64 MiB of HBM per device.

```python
import math
import jax
import jax.numpy as jnp
import numpy as np
from jax import lax

RANK = 64
COLS = 256
ROWS_DEV = 2048
LEVELS = 4
NODES = 15
SIDE0 = 1
N_ROWS = 32768
N_LEAF = 16


def draw_coeff_basis(key, part):
    level_scale = 1.0 / jnp.sqrt(ROWS_DEV * SIDE0 * 2.0 ** jnp.arange(LEVELS, dtype=jnp.float32))
    sample = jnp.clip(jax.random.normal(key, (LEVELS, RANK, N_ROWS), jnp.float32), -4.0, 4.0)
    return sample * level_scale[:, None, None]


def draw_node_inverse(key, part):
    order_two = 2 * RANK
    identity = jnp.eye(order_two, dtype=jnp.float32)
    first_key = jax.random.fold_in(key, 11)
    spread_part = jnp.clip(jax.random.normal(first_key, (NODES, order_two, order_two), jnp.float32), -4.0, 4.0)
    diag_gain = jnp.ones((NODES, order_two), jnp.float32)
    return identity[None] * diag_gain[:, :, None] + spread_part * (0.5 / jnp.sqrt(jnp.float32(order_two)))


def levels(stream_key, shape, pieces, smallest, top_value):
    factor_of = 1.0
    for dim, parts in pieces:
        heights = jax.random.uniform(jax.random.fold_in(jax.random.fold_in(stream_key, 6), dim), (parts,), jnp.float32, smallest / len(pieces), top_value / len(pieces))
        factor_of = factor_of * jnp.repeat(jnp.exp(heights), shape[dim] // parts).reshape((-1,) + (1,) * (len(shape) - 1 - dim))
    return factor_of


def length_profile(number_of, total, bound, slope):
    loads = [(1 << 20) // math.isqrt(grade ** slope) + 1 for grade in range(2, number_of + 1)]
    surplus, holding = total - bound - (number_of - 1), [1] * (number_of - 1)
    while surplus > 0:
        free = [i for i in range(number_of - 1) if holding[i] < bound]
        whole, budget = sum([loads[i] for i in free]), surplus
        for i in free:
            extra = min(bound - holding[i], max(1, budget * loads[i] // whole), surplus)
            holding[i] = holding[i] + extra
            surplus = surplus - extra
    return np.array([bound] + holding)


def uneven_parts(stream_key, amount, total, bound, skew):
    if amount == 2:
        one = jax.random.randint(stream_key, (), max(1, total - bound), min(bound, total - 1) + 1)
        return jnp.stack([one, total - one])
    sizes = jnp.asarray(length_profile(amount, total, bound, skew), jnp.int32)
    pairs = (amount - 1) // 2
    donor, sink = sizes[1:1 + 2 * pairs:2], sizes[2:2 + 2 * pairs:2]
    slack = jnp.minimum(donor - 1, bound - sink)
    shifted = jax.random.randint(jax.random.fold_in(stream_key, 1), (pairs,), 0, 1 << 20) % (slack + 1)
    sizes = sizes.at[1:1 + 2 * pairs:2].set(donor - shifted).at[2:2 + 2 * pairs:2].set(sink + shifted)
    return sizes[jax.random.permutation(jax.random.fold_in(stream_key, 2), amount)]


def normal_values(key, shape, scale, bound, pieces=(), kind=jnp.bfloat16):
    entries = jax.random.normal(key, shape, jnp.float32) * scale
    if len(pieces) > 0:
        entries = levels(key, shape, pieces, -0.22, 0.18) * entries
    return jnp.clip(entries, min=-bound, max=bound).astype(kind)


def setup_inputs(seed: int = 0, part: int = 0) -> dict:
    streams_of = jax.random.split(jax.random.key(seed), 7)
    own_keys = jax.random.split(jax.random.fold_in(streams_of[6], part), 7)
    right_side = normal_values(own_keys[0], (N_ROWS, COLS), 1.0, 6.0, ((0, 16),), jnp.float32)
    cotangent = normal_values(own_keys[1], (N_ROWS, COLS), 1.0, 6.0, ((0, 16),), jnp.float32)
    coeff_basis = draw_coeff_basis(jax.random.fold_in(jax.random.fold_in(streams_of[6], part), 71), part)
    saved_basis = normal_values(own_keys[3], (LEVELS, RANK, N_ROWS), 0.04, 0.24, ((2, 16),), jnp.float32)
    node_inverse = draw_node_inverse(jax.random.fold_in(jax.random.fold_in(streams_of[6], part), 71), part)
    leaf_rows = uneven_parts(own_keys[5], N_LEAF, N_LEAF * ROWS_DEV * 3 // 4, ROWS_DEV, 1).astype(jnp.int32)
    return {"right_side": right_side, "cotangent": cotangent, "coeff_basis": coeff_basis, "saved_basis": saved_basis, "node_inverse": node_inverse, "leaf_rows": leaf_rows}


def reference(right_side, cotangent, coeff_basis, saved_basis, node_inverse, leaf_rows):
    highest = lax.Precision.HIGHEST
    row_count = right_side.shape[0]
    within = jnp.arange(row_count, dtype=jnp.int32) % ROWS_DEV
    live_rows = (within < jnp.repeat(leaf_rows, ROWS_DEV)).astype(jnp.float32)
    current = right_side * live_rows[:, None]
    weights = cotangent * live_rows[:, None]
    saved_masked = saved_basis * live_rows[None, None, :]
    for height in range(LEVELS):
        side_count = 2 ** (LEVELS - height)
        side_rows = row_count // side_count
        basis_now = coeff_basis[height].reshape(RANK, side_count, side_rows)
        blocks = current.reshape(side_count, side_rows, COLS)
        coeffs = jnp.einsum('rsi,sic->src', basis_now, blocks, precision=highest)
        paired = coeffs.reshape(side_count // 2, 2 * RANK, COLS)
        offset = 2 ** LEVELS - side_count
        inverse = node_inverse[offset:offset + side_count // 2]
        mixture = jnp.einsum('nab,nbc->nac', inverse, paired, precision=highest).reshape(side_count, RANK, COLS)
        correction = jnp.einsum('rsi,src->sic', saved_masked[height].reshape(RANK, side_count, side_rows), mixture, precision=highest)
        current = current - correction.reshape(row_count, COLS)
    scale_factor = 1.0 / jnp.sqrt(jnp.float32(COLS))
    left_list = []
    right_list = []
    for height in range(LEVELS):
        side_count = 2 ** (LEVELS - height)
        side_rows = row_count // side_count
        basis_now = coeff_basis[height].reshape(RANK, side_count, side_rows)
        wblocks = weights.reshape(side_count, side_rows, COLS)
        fblocks = current.reshape(side_count, side_rows, COLS)
        k_sums = jnp.einsum('rsi,sic->src', basis_now, wblocks, precision=highest)
        l_sums = jnp.einsum('rsi,sic->src', basis_now, fblocks, precision=highest)
        k_swap = k_sums.reshape(side_count // 2, 2, RANK, COLS)[:, ::-1].reshape(side_count, RANK, COLS)
        l_swap = l_sums.reshape(side_count // 2, 2, RANK, COLS)[:, ::-1].reshape(side_count, RANK, COLS)
        left_now = jnp.einsum('src,sic->rsi', l_swap, wblocks, precision=highest) * scale_factor
        right_now = jnp.einsum('src,sic->rsi', k_swap, fblocks, precision=highest) * scale_factor
        left_list.append(left_now.reshape(RANK, row_count))
        right_list.append(right_now.reshape(RANK, row_count))
    grad_left = jnp.stack(left_list).astype(jnp.bfloat16)
    grad_right = jnp.stack(right_list).astype(jnp.bfloat16)
    return (current, grad_left, grad_right)
```

```python
import jax
import jax.numpy as jnp
from jax import lax
from jax.sharding import PartitionSpec as P

HI = lax.Precision.HIGHEST
MID = lax.Precision.HIGH


def swapped(value, bit):
    mask = 2**bit
    pairs = [(source, source ^ mask) for source in range(lax.axis_size("leaf"))]
    return lax.ppermute(value, "leaf", pairs)


def dot(a, b, dims=((1,), (0,)), precision=MID):
    return lax.dot_general(
        a, b, (dims, ((), ())), precision=precision, preferred_element_type=jnp.float32
    )


def tree(sums, weight_sums, gram, node_inverse, levels, rank, base):
    position = lax.axis_index("leaf")
    cols = sums.shape[1]
    half = cols // 2
    mine = jnp.right_shift(position, base) % 2
    s_own = lax.dynamic_slice_in_dim(sums, mine * half, half, 1)
    s_other = lax.dynamic_slice_in_dim(sums, (1 - mine) * half, half, 1)
    k_own = lax.dynamic_slice_in_dim(weight_sums, mine * half, half, 1)
    k_other = lax.dynamic_slice_in_dim(weight_sums, (1 - mine) * half, half, 1)
    g_own = gram
    z_list, c_list, k_list, row_list = [], [], [], []
    c_first, k_first, row_first = s_own[:rank], k_own[:rank], g_own[:rank]
    for height in range(levels):
        if height == 0:
            sent = jnp.concatenate([s_other, k_other, g_own], 1)
        else:
            sent = jnp.concatenate([s_own, k_own, g_own], 1)
        got = swapped(sent, base + height)
        s_sib, k_sib, g_sib = got[:, :half], got[:, half : 2 * half], got[:, 2 * half :]
        place = jnp.right_shift(position, base + height) % 2
        offset = 2**levels - 2 ** (levels - height)
        inverse = lax.dynamic_index_in_dim(
            node_inverse, offset + jnp.right_shift(position, base + height + 1), 0, keepdims=False
        )
        inverse = jnp.where(place == 0, inverse, jnp.roll(inverse, (rank, rank), (0, 1)))
        pair = jnp.concatenate([s_own[:rank], s_sib[:rank]], 0)
        z = dot(inverse, pair, precision=HI)
        z_list.append(z)
        c_list.append(s_sib[:rank])
        k_list.append(k_sib[:rank])
        row_list.append(g_sib[:rank])
        if height < levels - 1:
            response = jnp.concatenate([g_own[rank:, :rank], g_sib[rank:, :rank]], 1)
            s_own = s_own[rank:] + s_sib[rank:] - dot(response, z, precision=HI)
            k_own = k_own[rank:] + k_sib[rank:]
            g_own = (g_own + g_sib)[rank:, rank:]
    l_list = []
    for height in range(levels):
        z_chain = jnp.concatenate(
            [z_list[height][rank:]] + [z[:rank] for z in z_list[height + 1 :]], 0
        )
        l_list.append(c_list[height] - dot(row_list[height], z_chain, precision=HI))
    scale = 1.0 / jnp.sqrt(jnp.float32(cols))
    z_own = jnp.concatenate([z[:rank] for z in z_list], 0)
    l_first = c_first - dot(row_first, z_own, precision=HI)

    def pack(z_first, l_zero, k_zero):
        return jnp.concatenate(
            [z_first, z_own[rank:], l_zero * scale]
            + [l * scale for l in l_list[1:]]
            + [k_zero * scale]
            + [k * scale for k in k_list[1:]],
            0,
        )

    packed = pack(z_own[:rank], l_list[0], k_list[0])
    other = swapped(pack(z_list[0][rank:], l_first, k_first), base)
    full = jnp.where(
        mine == 0,
        jnp.concatenate([packed, other], 1),
        jnp.concatenate([other, packed], 1),
    )
    rows = levels * rank
    return full[:rows], full[rows : 2 * rows], full[2 * rows :]


def body(right_side, cotangent, coeff_basis, saved_basis, node_inverse, leaf_rows):
    row_count = right_side.shape[0]
    levels, rank = coeff_basis.shape[0], coeff_basis.shape[1]
    base = lax.axis_size("leaf").bit_length() - 1 - levels
    live = (jnp.arange(row_count, dtype=jnp.int32) < leaf_rows[0]).astype(jnp.float32)
    basis = coeff_basis.reshape(levels * rank, row_count) * live[None, :]
    saved = saved_basis.reshape(levels * rank, row_count)
    sums = dot(basis, right_side)
    weight_sums = dot(basis, cotangent)
    gram = dot(basis, saved, ((1,), (1,)))
    for bit in range(base):
        sums = sums + swapped(sums, bit)
        weight_sums = weight_sums + swapped(weight_sums, bit)
        gram = gram + swapped(gram, bit)
    z_own, l_sib, k_sib = tree(sums, weight_sums, gram, node_inverse, levels, rank, base)
    current = (right_side - dot(saved, z_own, ((0,), (0,)))) * live[:, None]
    left = dot(l_sib, cotangent, ((1,), (1,))) * live[None, :]
    right = dot(k_sib, current, ((1,), (1,)))
    shape = (levels, rank, row_count)
    return (
        current,
        left.astype(jnp.bfloat16).reshape(shape),
        right.astype(jnp.bfloat16).reshape(shape),
    )


def solution(mesh):
    in_specs = (
        P(("groups", "leaf"), None),
        P(("groups", "leaf"), None),
        P(None, None, ("groups", "leaf")),
        P(None, None, ("groups", "leaf")),
        P("groups", None, None),
        P(("groups", "leaf")),
    )
    out_specs = (
        P(("groups", "leaf"), None),
        P(None, None, ("groups", "leaf")),
        P(None, None, ("groups", "leaf")),
    )
    return jax.shard_map(body, mesh=mesh, in_specs=in_specs, out_specs=out_specs, check_vma=False)
```

```python
import functools
import math

import jax
import jax.numpy as jnp
from jax import lax
from jax.experimental import pallas as pl
from jax.experimental.pallas import tpu as pltpu
from jax.sharding import PartitionSpec as P

MESH = pl.DeviceIdType.MESH
HI = lax.Precision.HIGHEST
MID = lax.Precision.HIGH


def swapped(value, bit):
    mask = 2**bit
    pairs = [(source, source ^ mask) for source in range(lax.axis_size("leaf"))]
    return lax.ppermute(value, "leaf", pairs)


def dot(a, b, dims=((1,), (0,)), precision=MID):
    return lax.dot_general(
        a, b, (dims, ((), ())), precision=precision, preferred_element_type=jnp.float32
    )


def tree_kernel(
    levels, rank, base, s_ref, k_ref, g_ref, node_ref, z_out, l_out, k_out, *scratch
):
    inverse = scratch[0]
    own = [None] + [scratch[1 + 3 * n : 4 + 3 * n] for n in range(levels - 1)]
    start = 1 + 3 * (levels - 1)
    got = [scratch[start + 3 * n : start + 3 * n + 3] for n in range(levels)]
    start += 3 * levels
    packed, other, node_sem, send_sem, recv_sem = scratch[start:]
    cols = s_ref.shape[1]
    half = cols // 2
    position = lax.axis_index("leaf")

    def bit_of(height):
        return lax.rem(lax.div(position, 2 ** (base + height)), 2)

    def partner(height):
        return position + (1 - 2 * bit_of(height)) * 2 ** (base + height)

    fetches = []
    for height in range(levels):
        offset = 2**levels - 2 ** (levels - height)
        node = offset + lax.div(position, 2 ** (base + height + 1))
        fetch = pltpu.make_async_copy(node_ref.at[node], inverse.at[height], node_sem.at[height])
        fetch.start()
        fetches.append(fetch)

    barrier = pltpu.get_barrier_semaphore()
    for height in range(levels):
        pl.semaphore_signal(
            barrier, inc=1, device_id={"leaf": partner(height)}, device_id_type=MESH
        )
    pl.semaphore_wait(barrier, levels)

    def send(source, target, height, slot):
        copy = pltpu.make_async_remote_copy(
            src_ref=source,
            dst_ref=target,
            send_sem=send_sem.at[slot],
            recv_sem=recv_sem.at[slot],
            device_id={"leaf": partner(height)},
            device_id_type=MESH,
        )
        copy.start()
        return copy

    mine = bit_of(0)
    keep = pl.ds(pl.multiple_of(mine * half, half), half)
    give = pl.ds(pl.multiple_of((1 - mine) * half, half), half)
    s_now, k_now, g_now = s_ref.at[:, keep], k_ref.at[:, keep], g_ref
    copies = [
        send(s_ref.at[:, give], got[0][0], 0, 0),
        send(g_ref, got[0][1], 0, 1),
        send(k_ref.at[:, give], got[0][2], 0, 2),
    ]
    z_own, z_sib = [], []
    for height in range(levels):
        shift = rank * height - rank * height // 128 * 128
        s_got, g_got, k_got = got[height]
        copies[0].wait_recv()
        lower = bit_of(height) == 0
        here, there = s_now[:rank, :], s_got[:rank, :]
        pair = jnp.concatenate(
            [jnp.where(lower, here, there), jnp.where(lower, there, here)], 0
        )
        fetches[height].wait()
        z = dot(inverse[height], pair, precision=HI)
        z_own.append(jnp.where(lower, z[:rank], z[rank:]))
        z_sib.append(jnp.where(lower, z[rank:], z[:rank]))
        copies[1].wait_recv()
        if height < levels - 1:
            s_next, g_next, k_next = own[height + 1]
            block = slice(shift, shift + rank)
            s_next[...] = (
                s_now[rank:, :]
                + s_got[rank:, :]
                - dot(g_now[rank:, :][:, block], z_own[-1], precision=HI)
                - dot(g_got[rank:, :][:, block], z_sib[-1], precision=HI)
            )
            later = [send(s_next, got[height + 1][0], height + 1, 3 * height + 3)]
            skip = g_now.shape[1] - g_next.shape[1]
            g_next[...] = g_now[rank:, skip:] + g_got[rank:, skip:]
            later.append(send(g_next, got[height + 1][1], height + 1, 3 * height + 4))
        copies[2].wait_recv()
        if height < levels - 1:
            k_next[...] = k_now[rank:, :] + k_got[rank:, :]
            later.append(send(k_next, got[height + 1][2], height + 1, 3 * height + 5))
        for copy in copies:
            copy.wait_send()
        if height < levels - 1:
            copies = later
            s_now, g_now, k_now = own[height + 1]

    rows = levels * rank
    scale = 1.0 / math.sqrt(cols)
    z_all = jnp.concatenate(z_own, 0)
    packed[:rank, :] = z_sib[0]
    packed[rank:rows, :] = z_all[rank:]
    l_list = []
    for height in range(levels):
        shift = rank * height - rank * height // 128 * 128
        chain = jnp.concatenate([z_sib[height]] + z_own[height + 1 :], 0)
        row = got[height][1][:rank, :][:, shift:]
        l_list.append((got[height][0][:rank, :] - dot(row, chain, precision=HI)) * scale)
    l_first = (s_ref[:rank, keep] - dot(g_ref[:rank, :], z_all, precision=HI)) * scale
    packed[rows : rows + rank, :] = l_first
    packed[2 * rows : 2 * rows + rank, :] = k_ref[:rank, keep] * scale
    z_out[:, keep] = z_all
    for height in range(levels):
        part = slice(height * rank, (height + 1) * rank)
        k_part = got[height][2][:rank, :] * scale
        l_out[part, keep] = l_list[height]
        k_out[part, keep] = k_part
        if height > 0:
            packed[rows + height * rank : rows + (height + 1) * rank, :] = l_list[height]
            packed[2 * rows + height * rank : 2 * rows + (height + 1) * rank, :] = k_part
    last = send(packed, other, 0, 3 * levels)
    last.wait_recv()
    z_out[:, give] = other[:rows, :]
    l_out[:, give] = other[rows : 2 * rows, :]
    k_out[:, give] = other[2 * rows :, :]
    last.wait_send()


def tree(sums, weight_sums, gram, node_inverse, levels, rank, base):
    rows, cols = sums.shape
    half = cols // 2
    own, got = [], []
    for height in range(levels):
        left = rows - rank * height
        wide = rows - rank * height // 128 * 128
        group = [
            pltpu.VMEM((left, half), jnp.float32),
            pltpu.VMEM((left, wide), jnp.float32),
            pltpu.VMEM((left, half), jnp.float32),
        ]
        got += group
        if height > 0:
            own += group
    count = 3 * levels + 1
    vmem = pl.BlockSpec(memory_space=pltpu.VMEM)
    return pl.pallas_call(
        functools.partial(tree_kernel, levels, rank, base),
        out_shape=[jax.ShapeDtypeStruct((rows, cols), jnp.float32)] * 3,
        in_specs=[vmem] * 3 + [pl.BlockSpec(memory_space=pl.ANY)],
        out_specs=[vmem] * 3,
        scratch_shapes=[pltpu.VMEM((levels,) + node_inverse.shape[1:], jnp.float32)]
        + own
        + got
        + [
            pltpu.VMEM((3 * rows, half), jnp.float32),
            pltpu.VMEM((3 * rows, half), jnp.float32),
            pltpu.SemaphoreType.DMA((levels,)),
            pltpu.SemaphoreType.DMA((count,)),
            pltpu.SemaphoreType.DMA((count,)),
        ],
        compiler_params=pltpu.CompilerParams(collective_id=0, has_side_effects=True),
    )(sums, weight_sums, gram, node_inverse)


def body(right_side, cotangent, coeff_basis, saved_basis, node_inverse, leaf_rows):
    row_count = right_side.shape[0]
    levels, rank = coeff_basis.shape[0], coeff_basis.shape[1]
    base = lax.axis_size("leaf").bit_length() - 1 - levels
    live = (jnp.arange(row_count, dtype=jnp.int32) < leaf_rows[0]).astype(jnp.float32)
    basis = coeff_basis.reshape(levels * rank, row_count) * live[None, :]
    saved = saved_basis.reshape(levels * rank, row_count)
    sums = dot(basis, right_side)
    weight_sums = dot(basis, cotangent)
    gram = dot(basis, saved, ((1,), (1,)))
    for bit in range(base):
        sums = sums + swapped(sums, bit)
        weight_sums = weight_sums + swapped(weight_sums, bit)
        gram = gram + swapped(gram, bit)
    z_own, l_sib, k_sib = tree(sums, weight_sums, gram, node_inverse, levels, rank, base)
    current = (right_side - dot(saved, z_own, ((0,), (0,)))) * live[:, None]
    left = dot(l_sib, cotangent, ((1,), (1,))) * live[None, :]
    right = dot(k_sib, current, ((1,), (1,)))
    shape = (levels, rank, row_count)
    return (
        current,
        left.astype(jnp.bfloat16).reshape(shape),
        right.astype(jnp.bfloat16).reshape(shape),
    )


def solution(mesh):
    in_specs = (
        P(("groups", "leaf"), None),
        P(("groups", "leaf"), None),
        P(None, None, ("groups", "leaf")),
        P(None, None, ("groups", "leaf")),
        P("groups", None, None),
        P(("groups", "leaf")),
    )
    out_specs = (
        P(("groups", "leaf"), None),
        P(None, None, ("groups", "leaf")),
        P(None, None, ("groups", "leaf")),
    )
    return jax.shard_map(body, mesh=mesh, in_specs=in_specs, out_specs=out_specs, check_vma=False)
```

```python
import functools
import math

import jax
import jax.numpy as jnp
from jax import lax
from jax.experimental import pallas as pl
from jax.experimental.pallas import tpu as pltpu
from jax.sharding import PartitionSpec as P

MESH = pl.DeviceIdType.MESH
HI = lax.Precision.HIGHEST
TILE = 512


def swapped(value, bit):
    mask = 2**bit
    pairs = [(source, source ^ mask) for source in range(lax.axis_size("leaf"))]
    return lax.ppermute(value, "leaf", pairs)


def dot(a, b, dims=((1,), (0,)), precision=HI):
    return lax.dot_general(
        a, b, (dims, ((), ())), precision=precision, preferred_element_type=jnp.float32
    )


def tree_kernel(
    levels, rank, base, s_ref, k_ref, g_ref, node_ref, z_out, l_out, k_out, *scratch
):
    inverse = scratch[0]
    own = [None] + [scratch[1 + 3 * n : 4 + 3 * n] for n in range(levels - 1)]
    start = 1 + 3 * (levels - 1)
    got = [scratch[start + 3 * n : start + 3 * n + 3] for n in range(levels)]
    start += 3 * levels
    packed, other, node_sem, send_sem, recv_sem = scratch[start:]
    cols = s_ref.shape[1]
    half = cols // 2
    position = lax.axis_index("leaf")

    def bit_of(height):
        return lax.rem(lax.div(position, 2 ** (base + height)), 2)

    def partner(height):
        return position + (1 - 2 * bit_of(height)) * 2 ** (base + height)

    fetches = []
    for height in range(levels):
        offset = 2**levels - 2 ** (levels - height)
        node = offset + lax.div(position, 2 ** (base + height + 1))
        fetch = pltpu.make_async_copy(node_ref.at[node], inverse.at[height], node_sem.at[height])
        fetch.start()
        fetches.append(fetch)

    barrier = pltpu.get_barrier_semaphore()
    for height in range(levels):
        pl.semaphore_signal(
            barrier, inc=1, device_id={"leaf": partner(height)}, device_id_type=MESH
        )
    pl.semaphore_wait(barrier, levels)

    def send(source, target, height, slot):
        copy = pltpu.make_async_remote_copy(
            src_ref=source,
            dst_ref=target,
            send_sem=send_sem.at[slot],
            recv_sem=recv_sem.at[slot],
            device_id={"leaf": partner(height)},
            device_id_type=MESH,
        )
        copy.start()
        return copy

    mine = bit_of(0)
    keep = pl.ds(pl.multiple_of(mine * half, half), half)
    give = pl.ds(pl.multiple_of((1 - mine) * half, half), half)
    s_now, k_now, g_now = s_ref.at[:, keep], k_ref.at[:, keep], g_ref
    copies = [
        send(s_ref.at[:, give], got[0][0], 0, 0),
        send(g_ref, got[0][1], 0, 1),
        send(k_ref.at[:, give], got[0][2], 0, 2),
    ]
    z_own, z_sib = [], []
    for height in range(levels):
        shift = rank * height - rank * height // 128 * 128
        s_got, g_got, k_got = got[height]
        copies[0].wait_recv()
        lower = bit_of(height) == 0
        here, there = s_now[:rank, :], s_got[:rank, :]
        pair = jnp.concatenate(
            [jnp.where(lower, here, there), jnp.where(lower, there, here)], 0
        )
        fetches[height].wait()
        z = dot(inverse[height], pair, precision=HI)
        z_own.append(jnp.where(lower, z[:rank], z[rank:]))
        z_sib.append(jnp.where(lower, z[rank:], z[:rank]))
        copies[1].wait_recv()
        if height < levels - 1:
            s_next, g_next, k_next = own[height + 1]
            block = slice(shift, shift + rank)
            s_next[...] = (
                s_now[rank:, :]
                + s_got[rank:, :]
                - dot(g_now[rank:, :][:, block], z_own[-1], precision=HI)
                - dot(g_got[rank:, :][:, block], z_sib[-1], precision=HI)
            )
            later = [send(s_next, got[height + 1][0], height + 1, 3 * height + 3)]
            skip = g_now.shape[1] - g_next.shape[1]
            g_next[...] = g_now[rank:, skip:] + g_got[rank:, skip:]
            later.append(send(g_next, got[height + 1][1], height + 1, 3 * height + 4))
        copies[2].wait_recv()
        if height < levels - 1:
            k_next[...] = k_now[rank:, :] + k_got[rank:, :]
            later.append(send(k_next, got[height + 1][2], height + 1, 3 * height + 5))
        for copy in copies:
            copy.wait_send()
        if height < levels - 1:
            copies = later
            s_now, g_now, k_now = own[height + 1]

    rows = levels * rank
    scale = 1.0 / math.sqrt(cols)
    z_all = jnp.concatenate(z_own, 0)
    packed[:rank, :] = z_sib[0]
    packed[rank:rows, :] = z_all[rank:]
    l_list = []
    for height in range(levels):
        shift = rank * height - rank * height // 128 * 128
        chain = jnp.concatenate([z_sib[height]] + z_own[height + 1 :], 0)
        row = got[height][1][:rank, :][:, shift:]
        l_list.append((got[height][0][:rank, :] - dot(row, chain, precision=HI)) * scale)
    l_first = (s_ref[:rank, keep] - dot(g_ref[:rank, :], z_all, precision=HI)) * scale
    packed[rows : rows + rank, :] = l_first
    packed[2 * rows : 2 * rows + rank, :] = k_ref[:rank, keep] * scale
    z_out[:, keep] = z_all
    for height in range(levels):
        part = slice(height * rank, (height + 1) * rank)
        k_part = got[height][2][:rank, :] * scale
        l_out[part, keep] = l_list[height]
        k_out[part, keep] = k_part
        if height > 0:
            packed[rows + height * rank : rows + (height + 1) * rank, :] = l_list[height]
            packed[2 * rows + height * rank : 2 * rows + (height + 1) * rank, :] = k_part
    last = send(packed, other, 0, 3 * levels)
    last.wait_recv()
    z_out[:, give] = other[:rows, :]
    l_out[:, give] = other[rows : 2 * rows, :]
    k_out[:, give] = other[2 * rows :, :]
    last.wait_send()


def tree(sums, weight_sums, gram, node_inverse, levels, rank, base):
    rows, cols = sums.shape
    half = cols // 2
    own, got = [], []
    for height in range(levels):
        left = rows - rank * height
        wide = rows - rank * height // 128 * 128
        group = [
            pltpu.VMEM((left, half), jnp.float32),
            pltpu.VMEM((left, wide), jnp.float32),
            pltpu.VMEM((left, half), jnp.float32),
        ]
        got += group
        if height > 0:
            own += group
    count = 3 * levels + 1
    vmem = pl.BlockSpec(memory_space=pltpu.VMEM)
    return pl.pallas_call(
        functools.partial(tree_kernel, levels, rank, base),
        out_shape=[jax.ShapeDtypeStruct((rows, cols), jnp.float32)] * 3,
        in_specs=[vmem] * 3 + [pl.BlockSpec(memory_space=pl.ANY)],
        out_specs=[vmem] * 3,
        scratch_shapes=[pltpu.VMEM((levels,) + node_inverse.shape[1:], jnp.float32)]
        + own
        + got
        + [
            pltpu.VMEM((3 * rows, half), jnp.float32),
            pltpu.VMEM((3 * rows, half), jnp.float32),
            pltpu.SemaphoreType.DMA((levels,)),
            pltpu.SemaphoreType.DMA((count,)),
            pltpu.SemaphoreType.DMA((count,)),
        ],
        compiler_params=pltpu.CompilerParams(collective_id=0, has_side_effects=True),
    )(sums, weight_sums, gram, node_inverse)


def split(value):
    high = value.astype(jnp.bfloat16)
    return high, (value - high.astype(jnp.float32)).astype(jnp.bfloat16)


def triple(left, right, dims):
    def one(a, b):
        return lax.dot_general(a, b, (dims, ((), ())), preferred_element_type=jnp.float32)

    return one(left[0], right[1]) + one(left[1], right[0]) + one(left[0], right[0])


def lead_kernel(rows_ref, right_ref, cot_ref, basis_ref, saved_ref, s_ref, k_ref, g_ref):
    step = pl.program_id(0)
    tile = basis_ref.shape[1]
    place = step * tile + lax.broadcasted_iota(jnp.int32, (1, tile), 1)
    basis = split(jnp.where(place < rows_ref[0], basis_ref[...], 0.0))
    s_now = triple(basis, split(right_ref[...]), ((1,), (0,)))
    k_now = triple(basis, split(cot_ref[...]), ((1,), (0,)))
    g_now = triple(basis, split(saved_ref[...]), ((1,), (1,)))

    @pl.when(step == 0)
    def _():
        s_ref[...] = s_now
        k_ref[...] = k_now
        g_ref[...] = g_now

    @pl.when(step > 0)
    def _():
        s_ref[...] += s_now
        k_ref[...] += k_now
        g_ref[...] += g_now


def close_kernel(
    rows_ref, right_ref, cot_ref, saved_ref, z_ref, l_ref, k_ref, x_ref, left_ref, grad_ref
):
    tile = saved_ref.shape[1]
    first = pl.program_id(0) * tile
    down = first + lax.broadcasted_iota(jnp.int32, (tile, 1), 0)
    across = first + lax.broadcasted_iota(jnp.int32, (1, tile), 1)
    moved = triple(split(saved_ref[...]), split(z_ref[...]), ((0,), (0,)))
    solved = jnp.where(down < rows_ref[0], right_ref[...] - moved, 0.0)
    x_ref[...] = solved
    left = triple(split(l_ref[...]), split(cot_ref[...]), ((1,), (1,)))
    left_ref[...] = jnp.where(across < rows_ref[0], left, 0.0).astype(jnp.bfloat16)
    grad = triple(split(k_ref[...]), split(solved), ((1,), (1,)))
    grad_ref[...] = grad.astype(jnp.bfloat16)


def body(right_side, cotangent, coeff_basis, saved_basis, node_inverse, leaf_rows):
    row_count, cols = right_side.shape
    levels, rank = coeff_basis.shape[0], coeff_basis.shape[1]
    height = levels * rank
    base = lax.axis_size("leaf").bit_length() - 1 - levels
    basis = coeff_basis.reshape(height, row_count)
    saved = saved_basis.reshape(height, row_count)
    tile = math.gcd(row_count, TILE)
    grid = (row_count // tile,)
    count = pl.BlockSpec(memory_space=pltpu.SMEM)
    tall = pl.BlockSpec((tile, cols), lambda i: (i, 0))
    wide = pl.BlockSpec((height, tile), lambda i: (0, i))
    small = pl.BlockSpec((height, cols), lambda i: (0, 0))
    square = pl.BlockSpec((height, height), lambda i: (0, 0))
    sums, weight_sums, gram = pl.pallas_call(
        lead_kernel,
        grid=grid,
        out_shape=[
            jax.ShapeDtypeStruct((height, cols), jnp.float32),
            jax.ShapeDtypeStruct((height, cols), jnp.float32),
            jax.ShapeDtypeStruct((height, height), jnp.float32),
        ],
        in_specs=[count, tall, tall, wide, wide],
        out_specs=[small, small, square],
    )(leaf_rows, right_side, cotangent, basis, saved)
    for bit in range(base):
        sums = sums + swapped(sums, bit)
        weight_sums = weight_sums + swapped(weight_sums, bit)
        gram = gram + swapped(gram, bit)
    z_own, l_sib, k_sib = tree(sums, weight_sums, gram, node_inverse, levels, rank, base)
    current, left, right = pl.pallas_call(
        close_kernel,
        grid=grid,
        out_shape=[
            jax.ShapeDtypeStruct((row_count, cols), jnp.float32),
            jax.ShapeDtypeStruct((height, row_count), jnp.bfloat16),
            jax.ShapeDtypeStruct((height, row_count), jnp.bfloat16),
        ],
        in_specs=[count, tall, tall, wide, small, small, small],
        out_specs=[tall, wide, wide],
    )(leaf_rows, right_side, cotangent, saved, z_own, l_sib, k_sib)
    shape = (levels, rank, row_count)
    return current, left.reshape(shape), right.reshape(shape)


def solution(mesh):
    in_specs = (
        P(("groups", "leaf"), None),
        P(("groups", "leaf"), None),
        P(None, None, ("groups", "leaf")),
        P(None, None, ("groups", "leaf")),
        P("groups", None, None),
        P(("groups", "leaf")),
    )
    out_specs = (
        P(("groups", "leaf"), None),
        P(None, None, ("groups", "leaf")),
        P(None, None, ("groups", "leaf")),
    )
    return jax.shard_map(body, mesh=mesh, in_specs=in_specs, out_specs=out_specs, check_vma=False)
```

```python
import functools
import math

import jax
import jax.numpy as jnp
from jax import lax
from jax.experimental import pallas as pl
from jax.experimental.pallas import tpu as pltpu
from jax.sharding import PartitionSpec as P

MESH = pl.DeviceIdType.MESH
HI = lax.Precision.HIGHEST
TILE = 512


def swapped(value, bit):
    mask = 2**bit
    pairs = [(source, source ^ mask) for source in range(lax.axis_size("leaf"))]
    return lax.ppermute(value, "leaf", pairs)


def dot(a, b, dims=((1,), (0,)), precision=HI):
    return lax.dot_general(
        a, b, (dims, ((), ())), precision=precision, preferred_element_type=jnp.float32
    )


def tree_kernel(
    levels, rank, base, s_ref, k_ref, g_ref, node_ref, z_out, l_out, k_out, *scratch
):
    steps = [lambda: None] * 3
    tree_steps(
        levels, rank, base, steps, s_ref, k_ref, g_ref, node_ref, z_out, l_out, k_out, scratch
    )


def whole_kernel(
    levels,
    rank,
    tile,
    rows_ref,
    right_ref,
    cot_ref,
    basis_ref,
    saved_ref,
    node_ref,
    z_out,
    l_out,
    k_out,
    s_ref,
    k_ref,
    g_ref,
    right_in,
    cot_in,
    basis_in,
    saved_in,
    high_ref,
    low_ref,
    load_sem,
    *scratch,
):
    tiles = basis_ref.shape[1] // tile

    def load(source, target, kind, axis):
        copies = []
        for n in range(tiles):
            part = pl.ds(n * tile, tile)
            index = (part, slice(None)) if axis == 0 else (slice(None), part)
            copies.append(
                pltpu.make_async_copy(source.at[index], target.at[index], load_sem.at[kind, n])
            )
        return copies

    basis_loads = load(basis_ref, basis_in, 0, 1)
    saved_loads = load(saved_ref, saved_in, 1, 1)
    right_loads = load(right_ref, right_in, 2, 0)
    cot_loads = load(cot_ref, cot_in, 3, 0)
    for one, two in zip(basis_loads, saved_loads):
        one.start()
        two.start()
    for one in right_loads + cot_loads:
        one.start()

    def gram_step():
        total = None
        for n in range(tiles):
            part = slice(n * tile, (n + 1) * tile)
            place = n * tile + lax.broadcasted_iota(jnp.int32, (1, tile), 1)
            basis_loads[n].wait()
            high, low = split(jnp.where(place < rows_ref[0], basis_in[:, part], 0.0))
            high_ref[:, part] = high
            low_ref[:, part] = low
            saved_loads[n].wait()
            term = triple((high, low), split(saved_in[:, part]), ((1,), (1,)))
            total = term if total is None else total + term
        g_ref[...] = total

    def column_step(loads, source, target):
        total = None
        for n in range(tiles):
            part = slice(n * tile, (n + 1) * tile)
            loads[n].wait()
            basis = (high_ref[:, part], low_ref[:, part])
            term = triple(basis, split(source[part, :]), ((1,), (0,)))
            total = term if total is None else total + term
        target[...] = total

    steps = [
        gram_step,
        lambda: column_step(right_loads, right_in, s_ref),
        lambda: column_step(cot_loads, cot_in, k_ref),
    ]
    tree_steps(
        levels, rank, 0, steps, s_ref, k_ref, g_ref, node_ref, z_out, l_out, k_out, scratch
    )


def tree_steps(
    levels, rank, base, steps, s_ref, k_ref, g_ref, node_ref, z_out, l_out, k_out, scratch
):
    inverse = scratch[0]
    own = [None] + [scratch[1 + 3 * n : 4 + 3 * n] for n in range(levels - 1)]
    start = 1 + 3 * (levels - 1)
    got = [scratch[start + 3 * n : start + 3 * n + 3] for n in range(levels)]
    start += 3 * levels
    packed, other, node_sem, send_sem, recv_sem = scratch[start:]
    cols = s_ref.shape[1]
    half = cols // 2
    position = lax.axis_index("leaf")

    def bit_of(height):
        return lax.rem(lax.div(position, 2 ** (base + height)), 2)

    def partner(height):
        return position + (1 - 2 * bit_of(height)) * 2 ** (base + height)

    fetches = []
    for height in range(levels):
        offset = 2**levels - 2 ** (levels - height)
        node = offset + lax.div(position, 2 ** (base + height + 1))
        fetch = pltpu.make_async_copy(node_ref.at[node], inverse.at[height], node_sem.at[height])
        fetch.start()
        fetches.append(fetch)

    barrier = pltpu.get_barrier_semaphore()
    for height in range(levels):
        pl.semaphore_signal(
            barrier, inc=1, device_id={"leaf": partner(height)}, device_id_type=MESH
        )
    steps[0]()
    pl.semaphore_wait(barrier, levels)

    def send(source, target, height, slot):
        copy = pltpu.make_async_remote_copy(
            src_ref=source,
            dst_ref=target,
            send_sem=send_sem.at[slot],
            recv_sem=recv_sem.at[slot],
            device_id={"leaf": partner(height)},
            device_id_type=MESH,
        )
        copy.start()
        return copy

    mine = bit_of(0)
    keep = pl.ds(pl.multiple_of(mine * half, half), half)
    give = pl.ds(pl.multiple_of((1 - mine) * half, half), half)
    s_all = [s_ref.at[:, keep]] + [own[n][0] for n in range(1, levels)]
    g_all = [g_ref] + [own[n][1] for n in range(1, levels)]
    k_all = [k_ref.at[:, keep]] + [own[n][2] for n in range(1, levels)]
    sends = []

    def advance_gram(height, copy):
        copy.wait_recv()
        if height == levels - 1:
            return None
        g_now, g_got, g_next = g_all[height], got[height][1], g_all[height + 1]
        skip = g_now.shape[1] - g_next.shape[1]
        g_next[...] = g_now[rank:, skip:] + g_got[rank:, skip:]
        sends.append(send(g_next, got[height + 1][1], height + 1, 3 * height + 4))
        return sends[-1]

    g_copy = send(g_ref, got[0][1], 0, 1)
    sends.append(g_copy)
    steps[1]()
    s_copy = send(s_ref.at[:, give], got[0][0], 0, 0)
    sends.append(s_copy)
    g_copy = advance_gram(0, g_copy)
    steps[2]()
    k_copy = send(k_ref.at[:, give], got[0][2], 0, 2)
    sends.append(k_copy)
    z_own, z_sib = [], []
    for height in range(levels):
        shift = rank * height - rank * height // 128 * 128
        s_now, g_now, k_now = s_all[height], g_all[height], k_all[height]
        s_got, g_got, k_got = got[height]
        s_copy.wait_recv()
        lower = bit_of(height) == 0
        here, there = s_now[:rank, :], s_got[:rank, :]
        pair = jnp.concatenate(
            [jnp.where(lower, here, there), jnp.where(lower, there, here)], 0
        )
        fetches[height].wait()
        z = dot(inverse[height], pair, precision=HI)
        z_own.append(jnp.where(lower, z[:rank], z[rank:]))
        z_sib.append(jnp.where(lower, z[rank:], z[:rank]))
        if height < levels - 1:
            s_next, _, k_next = own[height + 1]
            block = slice(shift, shift + rank)
            s_next[...] = (
                s_now[rank:, :]
                + s_got[rank:, :]
                - dot(g_now[rank:, :][:, block], z_own[-1], precision=HI)
                - dot(g_got[rank:, :][:, block], z_sib[-1], precision=HI)
            )
            s_copy = send(s_next, got[height + 1][0], height + 1, 3 * height + 3)
            sends.append(s_copy)
            k_copy.wait_recv()
            k_next[...] = k_now[rank:, :] + k_got[rank:, :]
            k_copy = send(k_next, got[height + 1][2], height + 1, 3 * height + 5)
            sends.append(k_copy)
            g_copy = advance_gram(height + 1, g_copy)
    k_copy.wait_recv()
    for copy in sends:
        copy.wait_send()

    rows = levels * rank
    scale = 1.0 / math.sqrt(cols)
    z_all = jnp.concatenate(z_own, 0)
    packed[:rank, :] = z_sib[0]
    packed[rank:rows, :] = z_all[rank:]
    l_list = []
    for height in range(levels):
        shift = rank * height - rank * height // 128 * 128
        chain = jnp.concatenate([z_sib[height]] + z_own[height + 1 :], 0)
        row = got[height][1][:rank, :][:, shift:]
        l_list.append((got[height][0][:rank, :] - dot(row, chain, precision=HI)) * scale)
    l_first = (s_ref[:rank, keep] - dot(g_ref[:rank, :], z_all, precision=HI)) * scale
    packed[rows : rows + rank, :] = l_first
    packed[2 * rows : 2 * rows + rank, :] = k_ref[:rank, keep] * scale
    z_out[:, keep] = z_all
    for height in range(levels):
        part = slice(height * rank, (height + 1) * rank)
        k_part = got[height][2][:rank, :] * scale
        l_out[part, keep] = l_list[height]
        k_out[part, keep] = k_part
        if height > 0:
            packed[rows + height * rank : rows + (height + 1) * rank, :] = l_list[height]
            packed[2 * rows + height * rank : 2 * rows + (height + 1) * rank, :] = k_part
    last = send(packed, other, 0, 3 * levels)
    last.wait_recv()
    z_out[:, give] = other[:rows, :]
    l_out[:, give] = other[rows : 2 * rows, :]
    k_out[:, give] = other[2 * rows :, :]
    last.wait_send()


def tree_scratch(levels, rank, rows, cols, node_shape):
    half = cols // 2
    own, got = [], []
    for height in range(levels):
        left = rows - rank * height
        wide = rows - rank * height // 128 * 128
        group = [
            pltpu.VMEM((left, half), jnp.float32),
            pltpu.VMEM((left, wide), jnp.float32),
            pltpu.VMEM((left, half), jnp.float32),
        ]
        got += group
        if height > 0:
            own += group
    count = 3 * levels + 1
    return (
        [pltpu.VMEM((levels,) + node_shape, jnp.float32)]
        + own
        + got
        + [
            pltpu.VMEM((3 * rows, half), jnp.float32),
            pltpu.VMEM((3 * rows, half), jnp.float32),
            pltpu.SemaphoreType.DMA((levels,)),
            pltpu.SemaphoreType.DMA((count,)),
            pltpu.SemaphoreType.DMA((count,)),
        ]
    )


def tree(sums, weight_sums, gram, node_inverse, levels, rank, base):
    rows, cols = sums.shape
    vmem = pl.BlockSpec(memory_space=pltpu.VMEM)
    return pl.pallas_call(
        functools.partial(tree_kernel, levels, rank, base),
        out_shape=[jax.ShapeDtypeStruct((rows, cols), jnp.float32)] * 3,
        in_specs=[vmem] * 3 + [pl.BlockSpec(memory_space=pl.ANY)],
        out_specs=[vmem] * 3,
        scratch_shapes=tree_scratch(levels, rank, rows, cols, node_inverse.shape[1:]),
        compiler_params=pltpu.CompilerParams(collective_id=0, has_side_effects=True),
    )(sums, weight_sums, gram, node_inverse)


def whole_tree(leaf_rows, right_side, cotangent, basis, saved, node_inverse, levels, rank, tile):
    rows, depth = basis.shape
    cols = right_side.shape[1]
    vmem = pl.BlockSpec(memory_space=pltpu.VMEM)
    remote = pl.BlockSpec(memory_space=pl.ANY)
    return pl.pallas_call(
        functools.partial(whole_kernel, levels, rank, tile),
        out_shape=[jax.ShapeDtypeStruct((rows, cols), jnp.float32)] * 3,
        in_specs=[pl.BlockSpec(memory_space=pltpu.SMEM)] + [remote] * 5,
        out_specs=[vmem] * 3,
        scratch_shapes=[
            pltpu.VMEM((rows, cols), jnp.float32),
            pltpu.VMEM((rows, cols), jnp.float32),
            pltpu.VMEM((rows, rows), jnp.float32),
            pltpu.VMEM((depth, cols), jnp.float32),
            pltpu.VMEM((depth, cols), jnp.float32),
            pltpu.VMEM((rows, depth), jnp.float32),
            pltpu.VMEM((rows, depth), jnp.float32),
            pltpu.VMEM((rows, depth), jnp.bfloat16),
            pltpu.VMEM((rows, depth), jnp.bfloat16),
            pltpu.SemaphoreType.DMA((4, depth // tile)),
        ]
        + tree_scratch(levels, rank, rows, cols, node_inverse.shape[1:]),
        compiler_params=pltpu.CompilerParams(collective_id=0, has_side_effects=True),
    )(leaf_rows, right_side, cotangent, basis, saved, node_inverse)


def split(value):
    high = value.astype(jnp.bfloat16)
    return high, (value - high.astype(jnp.float32)).astype(jnp.bfloat16)


def triple(left, right, dims):
    def one(a, b):
        return lax.dot_general(a, b, (dims, ((), ())), preferred_element_type=jnp.float32)

    return one(left[0], right[1]) + one(left[1], right[0]) + one(left[0], right[0])


def lead_kernel(rows_ref, right_ref, cot_ref, basis_ref, saved_ref, s_ref, k_ref, g_ref):
    step = pl.program_id(0)
    tile = basis_ref.shape[1]
    place = step * tile + lax.broadcasted_iota(jnp.int32, (1, tile), 1)
    basis = split(jnp.where(place < rows_ref[0], basis_ref[...], 0.0))
    s_now = triple(basis, split(right_ref[...]), ((1,), (0,)))
    k_now = triple(basis, split(cot_ref[...]), ((1,), (0,)))
    g_now = triple(basis, split(saved_ref[...]), ((1,), (1,)))

    @pl.when(step == 0)
    def _():
        s_ref[...] = s_now
        k_ref[...] = k_now
        g_ref[...] = g_now

    @pl.when(step > 0)
    def _():
        s_ref[...] += s_now
        k_ref[...] += k_now
        g_ref[...] += g_now


def close_kernel(
    rows_ref, right_ref, cot_ref, saved_ref, z_ref, l_ref, k_ref, x_ref, left_ref, grad_ref
):
    tile = saved_ref.shape[1]
    first = pl.program_id(0) * tile
    down = first + lax.broadcasted_iota(jnp.int32, (tile, 1), 0)
    across = first + lax.broadcasted_iota(jnp.int32, (1, tile), 1)
    moved = triple(split(saved_ref[...]), split(z_ref[...]), ((0,), (0,)))
    solved = jnp.where(down < rows_ref[0], right_ref[...] - moved, 0.0)
    x_ref[...] = solved
    left = triple(split(l_ref[...]), split(cot_ref[...]), ((1,), (1,)))
    left_ref[...] = jnp.where(across < rows_ref[0], left, 0.0).astype(jnp.bfloat16)
    grad = triple(split(k_ref[...]), split(solved), ((1,), (1,)))
    grad_ref[...] = grad.astype(jnp.bfloat16)


def body(right_side, cotangent, coeff_basis, saved_basis, node_inverse, leaf_rows):
    row_count, cols = right_side.shape
    levels, rank = coeff_basis.shape[0], coeff_basis.shape[1]
    height = levels * rank
    base = lax.axis_size("leaf").bit_length() - 1 - levels
    basis = coeff_basis.reshape(height, row_count)
    saved = saved_basis.reshape(height, row_count)
    tile = math.gcd(row_count, TILE)
    grid = (row_count // tile,)
    count = pl.BlockSpec(memory_space=pltpu.SMEM)
    tall = pl.BlockSpec((tile, cols), lambda i: (i, 0))
    wide = pl.BlockSpec((height, tile), lambda i: (0, i))
    small = pl.BlockSpec((height, cols), lambda i: (0, 0))
    square = pl.BlockSpec((height, height), lambda i: (0, 0))
    if base == 0:
        z_own, l_sib, k_sib = whole_tree(
            leaf_rows, right_side, cotangent, basis, saved, node_inverse, levels, rank, tile
        )
    else:
        sums, weight_sums, gram = pl.pallas_call(
            lead_kernel,
            grid=grid,
            out_shape=[
                jax.ShapeDtypeStruct((height, cols), jnp.float32),
                jax.ShapeDtypeStruct((height, cols), jnp.float32),
                jax.ShapeDtypeStruct((height, height), jnp.float32),
            ],
            in_specs=[count, tall, tall, wide, wide],
            out_specs=[small, small, square],
        )(leaf_rows, right_side, cotangent, basis, saved)
        for bit in range(base):
            sums = sums + swapped(sums, bit)
            weight_sums = weight_sums + swapped(weight_sums, bit)
            gram = gram + swapped(gram, bit)
        z_own, l_sib, k_sib = tree(sums, weight_sums, gram, node_inverse, levels, rank, base)
    current, left, right = pl.pallas_call(
        close_kernel,
        grid=grid,
        out_shape=[
            jax.ShapeDtypeStruct((row_count, cols), jnp.float32),
            jax.ShapeDtypeStruct((height, row_count), jnp.bfloat16),
            jax.ShapeDtypeStruct((height, row_count), jnp.bfloat16),
        ],
        in_specs=[count, tall, tall, wide, small, small, small],
        out_specs=[tall, wide, wide],
    )(leaf_rows, right_side, cotangent, saved, z_own, l_sib, k_sib)
    shape = (levels, rank, row_count)
    return current, left.reshape(shape), right.reshape(shape)


def solution(mesh):
    in_specs = (
        P(("groups", "leaf"), None),
        P(("groups", "leaf"), None),
        P(None, None, ("groups", "leaf")),
        P(None, None, ("groups", "leaf")),
        P("groups", None, None),
        P(("groups", "leaf")),
    )
    out_specs = (
        P(("groups", "leaf"), None),
        P(None, None, ("groups", "leaf")),
        P(None, None, ("groups", "leaf")),
    )
    return jax.shard_map(body, mesh=mesh, in_specs=in_specs, out_specs=out_specs, check_vma=False)
```

```python
import functools
import math

import jax
import jax.numpy as jnp
from jax import lax
from jax.experimental import pallas as pl
from jax.experimental.pallas import tpu as pltpu
from jax.sharding import PartitionSpec as P

MESH = pl.DeviceIdType.MESH
TILE = 512


def swapped(value, bit):
    mask = 2**bit
    pairs = [(source, source ^ mask) for source in range(lax.axis_size("leaf"))]
    return lax.ppermute(value, "leaf", pairs)


def dot(a, b, dims=((1,), (0,))):
    return triple(split(a), split(b), dims)


def tree_kernel(
    levels, rank, base, s_ref, k_ref, g_ref, node_ref, z_out, l_out, k_out, *scratch
):
    steps = [lambda: None] * 3
    tree_steps(
        levels, rank, base, steps, s_ref, k_ref, g_ref, node_ref, z_out, l_out, k_out, scratch
    )


def whole_kernel(
    levels,
    rank,
    tile,
    rows_ref,
    right_ref,
    cot_ref,
    basis_ref,
    saved_ref,
    node_ref,
    z_out,
    l_out,
    k_out,
    s_ref,
    k_ref,
    g_ref,
    right_in,
    cot_in,
    basis_in,
    saved_in,
    high_ref,
    low_ref,
    load_sem,
    *scratch,
):
    tiles = basis_ref.shape[1] // tile

    def load(source, target, kind, axis):
        copies = []
        for n in range(tiles):
            part = pl.ds(n * tile, tile)
            index = (part, slice(None)) if axis == 0 else (slice(None), part)
            copies.append(
                pltpu.make_async_copy(source.at[index], target.at[index], load_sem.at[kind, n])
            )
        return copies

    basis_loads = load(basis_ref, basis_in, 0, 1)
    saved_loads = load(saved_ref, saved_in, 1, 1)
    right_loads = load(right_ref, right_in, 2, 0)
    cot_loads = load(cot_ref, cot_in, 3, 0)
    for one, two in zip(basis_loads, saved_loads):
        one.start()
        two.start()
    for one in right_loads + cot_loads:
        one.start()

    def gram_step():
        total = None
        for n in range(tiles):
            part = slice(n * tile, (n + 1) * tile)
            place = n * tile + lax.broadcasted_iota(jnp.int32, (1, tile), 1)
            basis_loads[n].wait()
            high, low = split(jnp.where(place < rows_ref[0], basis_in[:, part], 0.0))
            high_ref[:, part] = high
            low_ref[:, part] = low
            saved_loads[n].wait()
            term = triple((high, low), split(saved_in[:, part]), ((1,), (1,)))
            total = term if total is None else total + term
        g_ref[...] = total

    def column_step(loads, source, target):
        total = None
        for n in range(tiles):
            part = slice(n * tile, (n + 1) * tile)
            loads[n].wait()
            basis = (high_ref[:, part], low_ref[:, part])
            term = triple(basis, split(source[part, :]), ((1,), (0,)))
            total = term if total is None else total + term
        target[...] = total

    steps = [
        gram_step,
        lambda: column_step(right_loads, right_in, s_ref),
        lambda: column_step(cot_loads, cot_in, k_ref),
    ]
    tree_steps(
        levels, rank, 0, steps, s_ref, k_ref, g_ref, node_ref, z_out, l_out, k_out, scratch
    )


def tree_steps(
    levels, rank, base, steps, s_ref, k_ref, g_ref, node_ref, z_out, l_out, k_out, scratch
):
    inverse = scratch[0]
    own = [None] + [scratch[1 + 3 * n : 4 + 3 * n] for n in range(levels - 1)]
    start = 1 + 3 * (levels - 1)
    got = [scratch[start + 3 * n : start + 3 * n + 3] for n in range(levels)]
    start += 3 * levels
    packed, other, node_sem, send_sem, recv_sem = scratch[start:]
    cols = s_ref.shape[1]
    half = cols // 2
    position = lax.axis_index("leaf")

    def bit_of(height):
        return lax.rem(lax.div(position, 2 ** (base + height)), 2)

    def partner(height):
        return position + (1 - 2 * bit_of(height)) * 2 ** (base + height)

    fetches = []
    for height in range(levels):
        offset = 2**levels - 2 ** (levels - height)
        node = offset + lax.div(position, 2 ** (base + height + 1))
        fetch = pltpu.make_async_copy(node_ref.at[node], inverse.at[height], node_sem.at[height])
        fetch.start()
        fetches.append(fetch)

    barrier = pltpu.get_barrier_semaphore()
    for height in range(levels):
        pl.semaphore_signal(
            barrier, inc=1, device_id={"leaf": partner(height)}, device_id_type=MESH
        )
    steps[0]()
    pl.semaphore_wait(barrier, levels)

    def send(source, target, height, slot):
        copy = pltpu.make_async_remote_copy(
            src_ref=source,
            dst_ref=target,
            send_sem=send_sem.at[slot],
            recv_sem=recv_sem.at[slot],
            device_id={"leaf": partner(height)},
            device_id_type=MESH,
        )
        copy.start()
        return copy

    mine = bit_of(0)
    keep = pl.ds(pl.multiple_of(mine * half, half), half)
    give = pl.ds(pl.multiple_of((1 - mine) * half, half), half)
    s_all = [s_ref.at[:, keep]] + [own[n][0] for n in range(1, levels)]
    g_all = [g_ref] + [own[n][1] for n in range(1, levels)]
    k_all = [k_ref.at[:, keep]] + [own[n][2] for n in range(1, levels)]
    sends = []

    def advance_gram(height, copy):
        copy.wait_recv()
        if height == levels - 1:
            return None
        g_now, g_got, g_next = g_all[height], got[height][1], g_all[height + 1]
        skip = g_now.shape[1] - g_next.shape[1]
        g_next[...] = g_now[rank:, skip:] + g_got[rank:, skip:]
        sends.append(send(g_next, got[height + 1][1], height + 1, 3 * height + 4))
        return sends[-1]

    g_copy = send(g_ref, got[0][1], 0, 1)
    sends.append(g_copy)
    steps[1]()
    s_copy = send(s_ref.at[:, give], got[0][0], 0, 0)
    sends.append(s_copy)
    g_copy = advance_gram(0, g_copy)
    steps[2]()
    k_copy = send(k_ref.at[:, give], got[0][2], 0, 2)
    sends.append(k_copy)
    z_own, z_sib = [], []
    for height in range(levels):
        shift = rank * height - rank * height // 128 * 128
        s_now, g_now, k_now = s_all[height], g_all[height], k_all[height]
        s_got, g_got, k_got = got[height]
        s_copy.wait_recv()
        lower = bit_of(height) == 0
        here, there = s_now[:rank, :], s_got[:rank, :]
        pair = jnp.concatenate(
            [jnp.where(lower, here, there), jnp.where(lower, there, here)], 0
        )
        fetches[height].wait()
        z = dot(inverse[height], pair)
        z_own.append(jnp.where(lower, z[:rank], z[rank:]))
        z_sib.append(jnp.where(lower, z[rank:], z[:rank]))
        if height < levels - 1:
            s_next, _, k_next = own[height + 1]
            block = slice(shift, shift + rank)
            s_next[...] = (
                s_now[rank:, :]
                + s_got[rank:, :]
                - dot(g_now[rank:, :][:, block], z_own[-1])
                - dot(g_got[rank:, :][:, block], z_sib[-1])
            )
            s_copy = send(s_next, got[height + 1][0], height + 1, 3 * height + 3)
            sends.append(s_copy)
            k_copy.wait_recv()
            k_next[...] = k_now[rank:, :] + k_got[rank:, :]
            k_copy = send(k_next, got[height + 1][2], height + 1, 3 * height + 5)
            sends.append(k_copy)
            g_copy = advance_gram(height + 1, g_copy)
    rows = levels * rank
    scale = 1.0 / math.sqrt(cols)
    z_all = jnp.concatenate(z_own, 0)
    areas = [pl.ds(n * rows, rows) for n in range(3)]
    packed[:rank, :] = z_sib[0]
    packed[rank:rows, :] = z_all[rank:]
    last = [send(packed.at[areas[0]], other.at[areas[0]], 0, 3 * levels)]
    z_out[:, keep] = z_all
    l_first = (s_ref[:rank, keep] - dot(g_ref[:rank, :], z_all)) * scale
    packed[rows : rows + rank, :] = l_first
    for height in range(levels):
        shift = rank * height - rank * height // 128 * 128
        part = slice(height * rank, (height + 1) * rank)
        chain = jnp.concatenate([z_sib[height]] + z_own[height + 1 :], 0)
        row = got[height][1][:rank, :][:, shift:]
        l_part = (got[height][0][:rank, :] - dot(row, chain)) * scale
        l_out[part, keep] = l_part
        if height > 0:
            packed[rows + height * rank : rows + (height + 1) * rank, :] = l_part
    last.append(send(packed.at[areas[1]], other.at[areas[1]], 0, 3 * levels + 1))
    k_copy.wait_recv()
    packed[2 * rows : 2 * rows + rank, :] = k_ref[:rank, keep] * scale
    for height in range(levels):
        part = slice(height * rank, (height + 1) * rank)
        k_part = got[height][2][:rank, :] * scale
        k_out[part, keep] = k_part
        if height > 0:
            packed[2 * rows + height * rank : 2 * rows + (height + 1) * rank, :] = k_part
    last.append(send(packed.at[areas[2]], other.at[areas[2]], 0, 3 * levels + 2))
    for copy, target, area in zip(last, (z_out, l_out, k_out), areas):
        copy.wait_recv()
        target[:, give] = other[area, :]
    for copy in sends + last:
        copy.wait_send()


def tree_scratch(levels, rank, rows, cols, node_shape):
    half = cols // 2
    own, got = [], []
    for height in range(levels):
        left = rows - rank * height
        wide = rows - rank * height // 128 * 128
        group = [
            pltpu.VMEM((left, half), jnp.float32),
            pltpu.VMEM((left, wide), jnp.float32),
            pltpu.VMEM((left, half), jnp.float32),
        ]
        got += group
        if height > 0:
            own += group
    count = 3 * levels + 3
    return (
        [pltpu.VMEM((levels,) + node_shape, jnp.float32)]
        + own
        + got
        + [
            pltpu.VMEM((3 * rows, half), jnp.float32),
            pltpu.VMEM((3 * rows, half), jnp.float32),
            pltpu.SemaphoreType.DMA((levels,)),
            pltpu.SemaphoreType.DMA((count,)),
            pltpu.SemaphoreType.DMA((count,)),
        ]
    )


def tree(sums, weight_sums, gram, node_inverse, levels, rank, base):
    rows, cols = sums.shape
    vmem = pl.BlockSpec(memory_space=pltpu.VMEM)
    return pl.pallas_call(
        functools.partial(tree_kernel, levels, rank, base),
        out_shape=[jax.ShapeDtypeStruct((rows, cols), jnp.float32)] * 3,
        in_specs=[vmem] * 3 + [pl.BlockSpec(memory_space=pl.ANY)],
        out_specs=[vmem] * 3,
        scratch_shapes=tree_scratch(levels, rank, rows, cols, node_inverse.shape[1:]),
        compiler_params=pltpu.CompilerParams(collective_id=0, has_side_effects=True),
    )(sums, weight_sums, gram, node_inverse)


def whole_tree(leaf_rows, right_side, cotangent, basis, saved, node_inverse, levels, rank, tile):
    rows, depth = basis.shape
    cols = right_side.shape[1]
    vmem = pl.BlockSpec(memory_space=pltpu.VMEM)
    remote = pl.BlockSpec(memory_space=pl.ANY)
    return pl.pallas_call(
        functools.partial(whole_kernel, levels, rank, tile),
        out_shape=[jax.ShapeDtypeStruct((rows, cols), jnp.float32)] * 3,
        in_specs=[pl.BlockSpec(memory_space=pltpu.SMEM)] + [remote] * 5,
        out_specs=[vmem] * 3,
        scratch_shapes=[
            pltpu.VMEM((rows, cols), jnp.float32),
            pltpu.VMEM((rows, cols), jnp.float32),
            pltpu.VMEM((rows, rows), jnp.float32),
            pltpu.VMEM((depth, cols), jnp.float32),
            pltpu.VMEM((depth, cols), jnp.float32),
            pltpu.VMEM((rows, depth), jnp.float32),
            pltpu.VMEM((rows, depth), jnp.float32),
            pltpu.VMEM((rows, depth), jnp.bfloat16),
            pltpu.VMEM((rows, depth), jnp.bfloat16),
            pltpu.SemaphoreType.DMA((4, depth // tile)),
        ]
        + tree_scratch(levels, rank, rows, cols, node_inverse.shape[1:]),
        compiler_params=pltpu.CompilerParams(collective_id=0, has_side_effects=True),
    )(leaf_rows, right_side, cotangent, basis, saved, node_inverse)


def split(value):
    high = value.astype(jnp.bfloat16)
    return high, (value - high.astype(jnp.float32)).astype(jnp.bfloat16)


def triple(left, right, dims):
    def one(a, b):
        return lax.dot_general(a, b, (dims, ((), ())), preferred_element_type=jnp.float32)

    return one(left[0], right[1]) + one(left[1], right[0]) + one(left[0], right[0])


def lead_kernel(rows_ref, right_ref, cot_ref, basis_ref, saved_ref, s_ref, k_ref, g_ref):
    step = pl.program_id(0)
    tile = basis_ref.shape[1]
    place = step * tile + lax.broadcasted_iota(jnp.int32, (1, tile), 1)
    basis = split(jnp.where(place < rows_ref[0], basis_ref[...], 0.0))
    s_now = triple(basis, split(right_ref[...]), ((1,), (0,)))
    k_now = triple(basis, split(cot_ref[...]), ((1,), (0,)))
    g_now = triple(basis, split(saved_ref[...]), ((1,), (1,)))

    @pl.when(step == 0)
    def _():
        s_ref[...] = s_now
        k_ref[...] = k_now
        g_ref[...] = g_now

    @pl.when(step > 0)
    def _():
        s_ref[...] += s_now
        k_ref[...] += k_now
        g_ref[...] += g_now


def close_kernel(
    rows_ref, right_ref, cot_ref, saved_ref, z_ref, l_ref, k_ref, x_ref, left_ref, grad_ref
):
    tile = saved_ref.shape[1]
    first = pl.program_id(0) * tile
    down = first + lax.broadcasted_iota(jnp.int32, (tile, 1), 0)
    across = first + lax.broadcasted_iota(jnp.int32, (1, tile), 1)
    moved = triple(split(saved_ref[...]), split(z_ref[...]), ((0,), (0,)))
    solved = jnp.where(down < rows_ref[0], right_ref[...] - moved, 0.0)
    x_ref[...] = solved
    left = triple(split(l_ref[...]), split(cot_ref[...]), ((1,), (1,)))
    left_ref[...] = jnp.where(across < rows_ref[0], left, 0.0).astype(jnp.bfloat16)
    grad = triple(split(k_ref[...]), split(solved), ((1,), (1,)))
    grad_ref[...] = grad.astype(jnp.bfloat16)


def body(right_side, cotangent, coeff_basis, saved_basis, node_inverse, leaf_rows):
    row_count, cols = right_side.shape
    levels, rank = coeff_basis.shape[0], coeff_basis.shape[1]
    height = levels * rank
    base = lax.axis_size("leaf").bit_length() - 1 - levels
    basis = coeff_basis.reshape(height, row_count)
    saved = saved_basis.reshape(height, row_count)
    tile = math.gcd(row_count, TILE)
    grid = (row_count // tile,)
    count = pl.BlockSpec(memory_space=pltpu.SMEM)
    tall = pl.BlockSpec((tile, cols), lambda i: (i, 0))
    wide = pl.BlockSpec((height, tile), lambda i: (0, i))
    small = pl.BlockSpec((height, cols), lambda i: (0, 0))
    square = pl.BlockSpec((height, height), lambda i: (0, 0))
    if base == 0:
        z_own, l_sib, k_sib = whole_tree(
            leaf_rows, right_side, cotangent, basis, saved, node_inverse, levels, rank, tile
        )
    else:
        sums, weight_sums, gram = pl.pallas_call(
            lead_kernel,
            grid=grid,
            out_shape=[
                jax.ShapeDtypeStruct((height, cols), jnp.float32),
                jax.ShapeDtypeStruct((height, cols), jnp.float32),
                jax.ShapeDtypeStruct((height, height), jnp.float32),
            ],
            in_specs=[count, tall, tall, wide, wide],
            out_specs=[small, small, square],
        )(leaf_rows, right_side, cotangent, basis, saved)
        for bit in range(base):
            sums = sums + swapped(sums, bit)
            weight_sums = weight_sums + swapped(weight_sums, bit)
            gram = gram + swapped(gram, bit)
        z_own, l_sib, k_sib = tree(sums, weight_sums, gram, node_inverse, levels, rank, base)
    current, left, right = pl.pallas_call(
        close_kernel,
        grid=grid,
        out_shape=[
            jax.ShapeDtypeStruct((row_count, cols), jnp.float32),
            jax.ShapeDtypeStruct((height, row_count), jnp.bfloat16),
            jax.ShapeDtypeStruct((height, row_count), jnp.bfloat16),
        ],
        in_specs=[count, tall, tall, wide, small, small, small],
        out_specs=[tall, wide, wide],
    )(leaf_rows, right_side, cotangent, saved, z_own, l_sib, k_sib)
    shape = (levels, rank, row_count)
    return current, left.reshape(shape), right.reshape(shape)


def solution(mesh):
    in_specs = (
        P(("groups", "leaf"), None),
        P(("groups", "leaf"), None),
        P(None, None, ("groups", "leaf")),
        P(None, None, ("groups", "leaf")),
        P("groups", None, None),
        P(("groups", "leaf")),
    )
    out_specs = (
        P(("groups", "leaf"), None),
        P(None, None, ("groups", "leaf")),
        P(None, None, ("groups", "leaf")),
    )
    return jax.shard_map(body, mesh=mesh, in_specs=in_specs, out_specs=out_specs, check_vma=False)
```

```python
import functools
import math

import jax
import jax.numpy as jnp
from jax import lax
from jax.experimental import pallas as pl
from jax.experimental.pallas import tpu as pltpu
from jax.sharding import PartitionSpec as P

MESH = pl.DeviceIdType.MESH
TILE = 512


def swapped(value, bit):
    mask = 2**bit
    pairs = [(source, source ^ mask) for source in range(lax.axis_size("leaf"))]
    return lax.ppermute(value, "leaf", pairs)


def dot(a, b, dims=((1,), (0,))):
    return triple(split(a), split(b), dims)


def tree_kernel(
    levels, rank, base, s_ref, k_ref, g_ref, node_ref, z_out, l_out, k_out, *scratch
):
    steps = [lambda: None] * 3
    tree_steps(
        levels, rank, base, steps, s_ref, k_ref, g_ref, node_ref, z_out, l_out, k_out, scratch
    )


def whole_kernel(
    levels,
    rank,
    tile,
    rows_ref,
    right_ref,
    cot_ref,
    basis_ref,
    saved_ref,
    node_ref,
    z_out,
    l_out,
    k_out,
    s_ref,
    k_ref,
    g_ref,
    right_in,
    cot_in,
    basis_in,
    saved_in,
    high_ref,
    low_ref,
    load_sem,
    *scratch,
):
    tiles = basis_ref.shape[1] // tile

    def load(source, target, kind, axis):
        copies = []
        for n in range(tiles):
            part = pl.ds(n * tile, tile)
            index = (part, slice(None)) if axis == 0 else (slice(None), part)
            copies.append(
                pltpu.make_async_copy(source.at[index], target.at[index], load_sem.at[kind, n])
            )
        return copies

    basis_loads = load(basis_ref, basis_in, 0, 1)
    saved_loads = load(saved_ref, saved_in, 1, 1)
    right_loads = load(right_ref, right_in, 2, 0)
    cot_loads = load(cot_ref, cot_in, 3, 0)
    for one, two in zip(basis_loads, saved_loads):
        one.start()
        two.start()
    for one in right_loads + cot_loads:
        one.start()

    def gram_step():
        total = None
        for n in range(tiles):
            part = slice(n * tile, (n + 1) * tile)
            place = n * tile + lax.broadcasted_iota(jnp.int32, (1, tile), 1)
            basis_loads[n].wait()
            high, low = split(jnp.where(place < rows_ref[0], basis_in[:, part], 0.0))
            high_ref[:, part] = high
            low_ref[:, part] = low
            saved_loads[n].wait()
            term = triple((high, low), split(saved_in[:, part]), ((1,), (1,)))
            total = term if total is None else total + term
        g_ref[...] = total

    def column_step(loads, source, target):
        total = None
        for n in range(tiles):
            part = slice(n * tile, (n + 1) * tile)
            loads[n].wait()
            basis = (high_ref[:, part], low_ref[:, part])
            term = triple(basis, split(source[part, :]), ((1,), (0,)))
            total = term if total is None else total + term
        target[...] = total

    steps = [
        gram_step,
        lambda: column_step(right_loads, right_in, s_ref),
        lambda: column_step(cot_loads, cot_in, k_ref),
    ]
    tree_steps(
        levels, rank, 0, steps, s_ref, k_ref, g_ref, node_ref, z_out, l_out, k_out, scratch
    )


def tree_steps(
    levels, rank, base, steps, s_ref, k_ref, g_ref, node_ref, z_out, l_out, k_out, scratch
):
    inverse = scratch[0]
    own = [None] + [scratch[1 + 3 * n : 4 + 3 * n] for n in range(levels - 1)]
    start = 1 + 3 * (levels - 1)
    got = [scratch[start + 3 * n : start + 3 * n + 3] for n in range(levels)]
    start += 3 * levels
    packed, other, node_sem, send_sem, recv_sem = scratch[start:]
    cols = s_ref.shape[1]
    half = cols // 2
    position = lax.axis_index("leaf")

    def bit_of(height):
        return lax.rem(lax.div(position, 2 ** (base + height)), 2)

    def partner(height):
        return position + (1 - 2 * bit_of(height)) * 2 ** (base + height)

    fetches = []
    for height in range(levels):
        offset = 2**levels - 2 ** (levels - height)
        node = offset + lax.div(position, 2 ** (base + height + 1))
        fetch = pltpu.make_async_copy(node_ref.at[node], inverse.at[height], node_sem.at[height])
        fetch.start()
        fetches.append(fetch)

    barrier = pltpu.get_barrier_semaphore()
    for height in range(levels):
        pl.semaphore_signal(
            barrier, inc=1, device_id={"leaf": partner(height)}, device_id_type=MESH
        )
    steps[0]()
    pl.semaphore_wait(barrier, levels)

    def send(source, target, height, slot):
        copy = pltpu.make_async_remote_copy(
            src_ref=source,
            dst_ref=target,
            send_sem=send_sem.at[slot],
            recv_sem=recv_sem.at[slot],
            device_id={"leaf": partner(height)},
            device_id_type=MESH,
        )
        copy.start()
        return copy

    mine = bit_of(0)
    keep = pl.ds(pl.multiple_of(mine * half, half), half)
    give = pl.ds(pl.multiple_of((1 - mine) * half, half), half)
    s_all = [s_ref.at[:, keep]] + [own[n][0] for n in range(1, levels)]
    g_all = [g_ref] + [own[n][1] for n in range(1, levels)]
    k_all = [k_ref.at[:, keep]] + [own[n][2] for n in range(1, levels)]
    sends = []

    def half_rows(height):
        size = g_all[height].shape[0] // 2
        return pl.ds(pl.multiple_of(mine * size, 8), size)

    def advance_gram(height, copy):
        copy.wait_recv()
        if height == 1:
            area = got[1][1].at[half_rows(1), :]
            relay = send(area, area, 0, 3 * levels + 3)
            sends.append(relay)
            relay.wait_recv()
        if height == levels - 1:
            return None
        g_now, g_got, g_next = g_all[height], got[height][1], g_all[height + 1]
        skip = g_now.shape[1] - g_next.shape[1]
        g_next[...] = g_now[rank:, skip:] + g_got[rank:, skip:]
        source, target = g_next, got[height + 1][1]
        if height == 0:
            source, target = source.at[half_rows(1), :], target.at[half_rows(1), :]
        sends.append(send(source, target, height + 1, 3 * height + 4))
        return sends[-1]

    g_copy = send(g_ref, got[0][1], 0, 1)
    sends.append(g_copy)
    steps[1]()
    s_copy = send(s_ref.at[:, give], got[0][0], 0, 0)
    sends.append(s_copy)
    g_copy = advance_gram(0, g_copy)
    steps[2]()
    k_copy = send(k_ref.at[:, give], got[0][2], 0, 2)
    sends.append(k_copy)
    z_own, z_sib = [], []
    for height in range(levels):
        shift = rank * height - rank * height // 128 * 128
        s_now, g_now, k_now = s_all[height], g_all[height], k_all[height]
        s_got, g_got, k_got = got[height]
        s_copy.wait_recv()
        lower = bit_of(height) == 0
        here, there = s_now[:rank, :], s_got[:rank, :]
        pair = jnp.concatenate(
            [jnp.where(lower, here, there), jnp.where(lower, there, here)], 0
        )
        fetches[height].wait()
        z = dot(inverse[height], pair)
        z_own.append(jnp.where(lower, z[:rank], z[rank:]))
        z_sib.append(jnp.where(lower, z[rank:], z[:rank]))
        if height < levels - 1:
            s_next, _, k_next = own[height + 1]
            block = slice(shift, shift + rank)
            s_next[...] = (
                s_now[rank:, :]
                + s_got[rank:, :]
                - dot(g_now[rank:, :][:, block], z_own[-1])
                - dot(g_got[rank:, :][:, block], z_sib[-1])
            )
            s_copy = send(s_next, got[height + 1][0], height + 1, 3 * height + 3)
            sends.append(s_copy)
            k_copy.wait_recv()
            k_next[...] = k_now[rank:, :] + k_got[rank:, :]
            k_copy = send(k_next, got[height + 1][2], height + 1, 3 * height + 5)
            sends.append(k_copy)
            g_copy = advance_gram(height + 1, g_copy)
    rows = levels * rank
    scale = 1.0 / math.sqrt(cols)
    z_all = jnp.concatenate(z_own, 0)
    areas = [pl.ds(n * rows, rows) for n in range(3)]
    packed[:rank, :] = z_sib[0]
    packed[rank:rows, :] = z_all[rank:]
    last = [send(packed.at[areas[0]], other.at[areas[0]], 0, 3 * levels)]
    z_out[:, keep] = z_all
    l_first = (s_ref[:rank, keep] - dot(g_ref[:rank, :], z_all)) * scale
    packed[rows : rows + rank, :] = l_first
    for height in range(levels):
        shift = rank * height - rank * height // 128 * 128
        part = slice(height * rank, (height + 1) * rank)
        chain = jnp.concatenate([z_sib[height]] + z_own[height + 1 :], 0)
        row = got[height][1][:rank, :][:, shift:]
        l_part = (got[height][0][:rank, :] - dot(row, chain)) * scale
        l_out[part, keep] = l_part
        if height > 0:
            packed[rows + height * rank : rows + (height + 1) * rank, :] = l_part
    last.append(send(packed.at[areas[1]], other.at[areas[1]], 0, 3 * levels + 1))
    k_copy.wait_recv()
    packed[2 * rows : 2 * rows + rank, :] = k_ref[:rank, keep] * scale
    for height in range(levels):
        part = slice(height * rank, (height + 1) * rank)
        k_part = got[height][2][:rank, :] * scale
        k_out[part, keep] = k_part
        if height > 0:
            packed[2 * rows + height * rank : 2 * rows + (height + 1) * rank, :] = k_part
    last.append(send(packed.at[areas[2]], other.at[areas[2]], 0, 3 * levels + 2))
    for copy, target, area in zip(last, (z_out, l_out, k_out), areas):
        copy.wait_recv()
        target[:, give] = other[area, :]
    for copy in sends + last:
        copy.wait_send()


def tree_scratch(levels, rank, rows, cols, node_shape):
    half = cols // 2
    own, got = [], []
    for height in range(levels):
        left = rows - rank * height
        wide = rows - rank * height // 128 * 128
        group = [
            pltpu.VMEM((left, half), jnp.float32),
            pltpu.VMEM((left, wide), jnp.float32),
            pltpu.VMEM((left, half), jnp.float32),
        ]
        got += group
        if height > 0:
            own += group
    count = 3 * levels + 4
    return (
        [pltpu.VMEM((levels,) + node_shape, jnp.float32)]
        + own
        + got
        + [
            pltpu.VMEM((3 * rows, half), jnp.float32),
            pltpu.VMEM((3 * rows, half), jnp.float32),
            pltpu.SemaphoreType.DMA((levels,)),
            pltpu.SemaphoreType.DMA((count,)),
            pltpu.SemaphoreType.DMA((count,)),
        ]
    )


def tree(sums, weight_sums, gram, node_inverse, levels, rank, base):
    rows, cols = sums.shape
    vmem = pl.BlockSpec(memory_space=pltpu.VMEM)
    return pl.pallas_call(
        functools.partial(tree_kernel, levels, rank, base),
        out_shape=[jax.ShapeDtypeStruct((rows, cols), jnp.float32)] * 3,
        in_specs=[vmem] * 3 + [pl.BlockSpec(memory_space=pl.ANY)],
        out_specs=[vmem] * 3,
        scratch_shapes=tree_scratch(levels, rank, rows, cols, node_inverse.shape[1:]),
        compiler_params=pltpu.CompilerParams(collective_id=0, has_side_effects=True),
    )(sums, weight_sums, gram, node_inverse)


def whole_tree(leaf_rows, right_side, cotangent, basis, saved, node_inverse, levels, rank, tile):
    rows, depth = basis.shape
    cols = right_side.shape[1]
    vmem = pl.BlockSpec(memory_space=pltpu.VMEM)
    remote = pl.BlockSpec(memory_space=pl.ANY)
    return pl.pallas_call(
        functools.partial(whole_kernel, levels, rank, tile),
        out_shape=[jax.ShapeDtypeStruct((rows, cols), jnp.float32)] * 3,
        in_specs=[pl.BlockSpec(memory_space=pltpu.SMEM)] + [remote] * 5,
        out_specs=[vmem] * 3,
        scratch_shapes=[
            pltpu.VMEM((rows, cols), jnp.float32),
            pltpu.VMEM((rows, cols), jnp.float32),
            pltpu.VMEM((rows, rows), jnp.float32),
            pltpu.VMEM((depth, cols), jnp.float32),
            pltpu.VMEM((depth, cols), jnp.float32),
            pltpu.VMEM((rows, depth), jnp.float32),
            pltpu.VMEM((rows, depth), jnp.float32),
            pltpu.VMEM((rows, depth), jnp.bfloat16),
            pltpu.VMEM((rows, depth), jnp.bfloat16),
            pltpu.SemaphoreType.DMA((4, depth // tile)),
        ]
        + tree_scratch(levels, rank, rows, cols, node_inverse.shape[1:]),
        compiler_params=pltpu.CompilerParams(collective_id=0, has_side_effects=True),
    )(leaf_rows, right_side, cotangent, basis, saved, node_inverse)


def split(value):
    high = value.astype(jnp.bfloat16)
    return high, (value - high.astype(jnp.float32)).astype(jnp.bfloat16)


def triple(left, right, dims):
    def one(a, b):
        return lax.dot_general(a, b, (dims, ((), ())), preferred_element_type=jnp.float32)

    return one(left[0], right[1]) + one(left[1], right[0]) + one(left[0], right[0])


def lead_kernel(rows_ref, right_ref, cot_ref, basis_ref, saved_ref, s_ref, k_ref, g_ref):
    step = pl.program_id(0)
    tile = basis_ref.shape[1]
    place = step * tile + lax.broadcasted_iota(jnp.int32, (1, tile), 1)
    basis = split(jnp.where(place < rows_ref[0], basis_ref[...], 0.0))
    s_now = triple(basis, split(right_ref[...]), ((1,), (0,)))
    k_now = triple(basis, split(cot_ref[...]), ((1,), (0,)))
    g_now = triple(basis, split(saved_ref[...]), ((1,), (1,)))

    @pl.when(step == 0)
    def _():
        s_ref[...] = s_now
        k_ref[...] = k_now
        g_ref[...] = g_now

    @pl.when(step > 0)
    def _():
        s_ref[...] += s_now
        k_ref[...] += k_now
        g_ref[...] += g_now


def close_kernel(
    rows_ref, right_ref, cot_ref, saved_ref, z_ref, l_ref, k_ref, x_ref, left_ref, grad_ref
):
    tile = saved_ref.shape[1]
    first = pl.program_id(0) * tile
    down = first + lax.broadcasted_iota(jnp.int32, (tile, 1), 0)
    across = first + lax.broadcasted_iota(jnp.int32, (1, tile), 1)
    moved = triple(split(saved_ref[...]), split(z_ref[...]), ((0,), (0,)))
    solved = jnp.where(down < rows_ref[0], right_ref[...] - moved, 0.0)
    x_ref[...] = solved
    left = triple(split(l_ref[...]), split(cot_ref[...]), ((1,), (1,)))
    left_ref[...] = jnp.where(across < rows_ref[0], left, 0.0).astype(jnp.bfloat16)
    grad = triple(split(k_ref[...]), split(solved), ((1,), (1,)))
    grad_ref[...] = grad.astype(jnp.bfloat16)


def body(right_side, cotangent, coeff_basis, saved_basis, node_inverse, leaf_rows):
    row_count, cols = right_side.shape
    levels, rank = coeff_basis.shape[0], coeff_basis.shape[1]
    height = levels * rank
    base = lax.axis_size("leaf").bit_length() - 1 - levels
    basis = coeff_basis.reshape(height, row_count)
    saved = saved_basis.reshape(height, row_count)
    tile = math.gcd(row_count, TILE)
    grid = (row_count // tile,)
    count = pl.BlockSpec(memory_space=pltpu.SMEM)
    tall = pl.BlockSpec((tile, cols), lambda i: (i, 0))
    wide = pl.BlockSpec((height, tile), lambda i: (0, i))
    small = pl.BlockSpec((height, cols), lambda i: (0, 0))
    square = pl.BlockSpec((height, height), lambda i: (0, 0))
    if base == 0:
        z_own, l_sib, k_sib = whole_tree(
            leaf_rows, right_side, cotangent, basis, saved, node_inverse, levels, rank, tile
        )
    else:
        sums, weight_sums, gram = pl.pallas_call(
            lead_kernel,
            grid=grid,
            out_shape=[
                jax.ShapeDtypeStruct((height, cols), jnp.float32),
                jax.ShapeDtypeStruct((height, cols), jnp.float32),
                jax.ShapeDtypeStruct((height, height), jnp.float32),
            ],
            in_specs=[count, tall, tall, wide, wide],
            out_specs=[small, small, square],
        )(leaf_rows, right_side, cotangent, basis, saved)
        for bit in range(base):
            sums = sums + swapped(sums, bit)
            weight_sums = weight_sums + swapped(weight_sums, bit)
            gram = gram + swapped(gram, bit)
        z_own, l_sib, k_sib = tree(sums, weight_sums, gram, node_inverse, levels, rank, base)
    current, left, right = pl.pallas_call(
        close_kernel,
        grid=grid,
        out_shape=[
            jax.ShapeDtypeStruct((row_count, cols), jnp.float32),
            jax.ShapeDtypeStruct((height, row_count), jnp.bfloat16),
            jax.ShapeDtypeStruct((height, row_count), jnp.bfloat16),
        ],
        in_specs=[count, tall, tall, wide, small, small, small],
        out_specs=[tall, wide, wide],
    )(leaf_rows, right_side, cotangent, saved, z_own, l_sib, k_sib)
    shape = (levels, rank, row_count)
    return current, left.reshape(shape), right.reshape(shape)


def solution(mesh):
    in_specs = (
        P(("groups", "leaf"), None),
        P(("groups", "leaf"), None),
        P(None, None, ("groups", "leaf")),
        P(None, None, ("groups", "leaf")),
        P("groups", None, None),
        P(("groups", "leaf")),
    )
    out_specs = (
        P(("groups", "leaf"), None),
        P(None, None, ("groups", "leaf")),
        P(None, None, ("groups", "leaf")),
    )
    return jax.shard_map(body, mesh=mesh, in_specs=in_specs, out_specs=out_specs, check_vma=False)
```

```python
import functools
import math

import jax
import jax.numpy as jnp
from jax import lax
from jax.experimental import pallas as pl
from jax.experimental.pallas import tpu as pltpu
from jax.sharding import PartitionSpec as P

MESH = pl.DeviceIdType.MESH
TILE = 512


def swapped(value, bit):
    mask = 2**bit
    pairs = [(source, source ^ mask) for source in range(lax.axis_size("leaf"))]
    return lax.ppermute(value, "leaf", pairs)


def dot(a, b, dims=((1,), (0,))):
    return triple(split(a), split(b), dims)


def tree_kernel(
    levels, rank, base, s_ref, k_ref, g_ref, node_ref, z_out, l_out, k_out, *scratch
):
    steps = [lambda: None] * 3
    tree_steps(
        levels, rank, base, steps, s_ref, k_ref, g_ref, node_ref, z_out, l_out, k_out, scratch
    )


def whole_kernel(
    levels,
    rank,
    tile,
    rows_ref,
    right_ref,
    cot_ref,
    basis_ref,
    saved_ref,
    node_ref,
    z_out,
    l_out,
    k_out,
    s_ref,
    k_ref,
    g_ref,
    right_in,
    cot_in,
    basis_in,
    saved_in,
    high_ref,
    low_ref,
    load_sem,
    *scratch,
):
    tiles = basis_ref.shape[1] // tile

    def load(source, target, kind, axis):
        copies = []
        for n in range(tiles):
            part = pl.ds(n * tile, tile)
            index = (part, slice(None)) if axis == 0 else (slice(None), part)
            copies.append(
                pltpu.make_async_copy(source.at[index], target.at[index], load_sem.at[kind, n])
            )
        return copies

    basis_loads = load(basis_ref, basis_in, 0, 1)
    saved_loads = load(saved_ref, saved_in, 1, 1)
    right_loads = load(right_ref, right_in, 2, 0)
    cot_loads = load(cot_ref, cot_in, 3, 0)
    for one, two in zip(basis_loads, saved_loads):
        one.start()
        two.start()
    for one in right_loads + cot_loads:
        one.start()

    def gram_step():
        total = None
        for n in range(tiles):
            part = slice(n * tile, (n + 1) * tile)
            place = n * tile + lax.broadcasted_iota(jnp.int32, (1, tile), 1)
            basis_loads[n].wait()
            high, low = split(jnp.where(place < rows_ref[0], basis_in[:, part], 0.0))
            high_ref[:, part] = high
            low_ref[:, part] = low
            saved_loads[n].wait()
            term = triple((high, low), split(saved_in[:, part]), ((1,), (1,)))
            total = term if total is None else total + term
        g_ref[...] = total

    def column_step(loads, source, target):
        total = None
        for n in range(tiles):
            part = slice(n * tile, (n + 1) * tile)
            loads[n].wait()
            basis = (high_ref[:, part], low_ref[:, part])
            term = triple(basis, split(source[part, :]), ((1,), (0,)))
            total = term if total is None else total + term
        target[...] = total

    steps = [
        gram_step,
        lambda: column_step(right_loads, right_in, s_ref),
        lambda: column_step(cot_loads, cot_in, k_ref),
    ]
    tree_steps(
        levels, rank, 0, steps, s_ref, k_ref, g_ref, node_ref, z_out, l_out, k_out, scratch
    )


def tree_steps(
    levels, rank, base, steps, s_ref, k_ref, g_ref, node_ref, z_out, l_out, k_out, scratch
):
    inverse = scratch[0]
    own = [None] + [scratch[1 + 3 * n : 4 + 3 * n] for n in range(levels - 1)]
    start = 1 + 3 * (levels - 1)
    got = [scratch[start + 3 * n : start + 3 * n + 3] for n in range(levels)]
    start += 3 * levels
    packed, other, node_sem, send_sem, recv_sem = scratch[start:]
    cols = s_ref.shape[1]
    half = cols // 2
    position = lax.axis_index("leaf")

    def bit_of(height):
        return lax.rem(lax.div(position, 2 ** (base + height)), 2)

    def partner(height):
        return position + (1 - 2 * bit_of(height)) * 2 ** (base + height)

    fetches = []
    for height in range(levels):
        offset = 2**levels - 2 ** (levels - height)
        node = offset + lax.div(position, 2 ** (base + height + 1))
        fetch = pltpu.make_async_copy(node_ref.at[node], inverse.at[height], node_sem.at[height])
        fetch.start()
        fetches.append(fetch)

    barrier = pltpu.get_barrier_semaphore()
    for height in range(levels):
        pl.semaphore_signal(
            barrier, inc=1, device_id={"leaf": partner(height)}, device_id_type=MESH
        )
    steps[0]()
    pl.semaphore_wait(barrier, levels)

    def send(source, target, height, slot):
        copy = pltpu.make_async_remote_copy(
            src_ref=source,
            dst_ref=target,
            send_sem=send_sem.at[slot],
            recv_sem=recv_sem.at[slot],
            device_id={"leaf": partner(height)},
            device_id_type=MESH,
        )
        copy.start()
        return copy

    mine = bit_of(0)
    keep = pl.ds(pl.multiple_of(mine * half, half), half)
    give = pl.ds(pl.multiple_of((1 - mine) * half, half), half)
    s_all = [s_ref.at[:, keep]] + [own[n][0] for n in range(1, levels)]
    g_all = [g_ref] + [own[n][1] for n in range(1, levels)]
    k_all = [k_ref.at[:, keep]] + [own[n][2] for n in range(1, levels)]
    sends = []

    def half_rows(height):
        size = g_all[height].shape[0] // 2
        return pl.ds(pl.multiple_of(mine * size, 8), size)

    def advance_gram(height, copy):
        copy.wait_recv()
        if 0 < height < levels - 1:
            area = got[height][1].at[half_rows(height), :]
            relay = send(area, area, 0, 3 * levels + 2 + height)
            sends.append(relay)
            relay.wait_recv()
        if height == levels - 1:
            return None
        g_now, g_got, g_next = g_all[height], got[height][1], g_all[height + 1]
        skip = g_now.shape[1] - g_next.shape[1]
        g_next[...] = g_now[rank:, skip:] + g_got[rank:, skip:]
        source, target = g_next, got[height + 1][1]
        if height < levels - 2:
            area = half_rows(height + 1)
            source, target = source.at[area, :], target.at[area, :]
        sends.append(send(source, target, height + 1, 3 * height + 4))
        return sends[-1]

    g_copy = send(g_ref, got[0][1], 0, 1)
    sends.append(g_copy)
    steps[1]()
    s_copy = send(s_ref.at[:, give], got[0][0], 0, 0)
    sends.append(s_copy)
    g_copy = advance_gram(0, g_copy)
    steps[2]()
    k_copy = send(k_ref.at[:, give], got[0][2], 0, 2)
    sends.append(k_copy)
    z_own, z_sib = [], []
    for height in range(levels):
        shift = rank * height - rank * height // 128 * 128
        s_now, g_now, k_now = s_all[height], g_all[height], k_all[height]
        s_got, g_got, k_got = got[height]
        s_copy.wait_recv()
        lower = bit_of(height) == 0
        here, there = s_now[:rank, :], s_got[:rank, :]
        pair = jnp.concatenate(
            [jnp.where(lower, here, there), jnp.where(lower, there, here)], 0
        )
        fetches[height].wait()
        z = dot(inverse[height], pair)
        z_own.append(jnp.where(lower, z[:rank], z[rank:]))
        z_sib.append(jnp.where(lower, z[rank:], z[:rank]))
        if height < levels - 1:
            s_next, _, k_next = own[height + 1]
            block = slice(shift, shift + rank)
            s_next[...] = (
                s_now[rank:, :]
                + s_got[rank:, :]
                - dot(g_now[rank:, :][:, block], z_own[-1])
                - dot(g_got[rank:, :][:, block], z_sib[-1])
            )
            s_copy = send(s_next, got[height + 1][0], height + 1, 3 * height + 3)
            sends.append(s_copy)
            k_copy.wait_recv()
            k_next[...] = k_now[rank:, :] + k_got[rank:, :]
            k_copy = send(k_next, got[height + 1][2], height + 1, 3 * height + 5)
            sends.append(k_copy)
            g_copy = advance_gram(height + 1, g_copy)
    rows = levels * rank
    scale = 1.0 / math.sqrt(cols)
    z_all = jnp.concatenate(z_own, 0)
    areas = [pl.ds(n * rows, rows) for n in range(3)]
    packed[:rank, :] = z_sib[0]
    packed[rank:rows, :] = z_all[rank:]
    last = [send(packed.at[areas[0]], other.at[areas[0]], 0, 3 * levels)]
    z_out[:, keep] = z_all
    l_first = (s_ref[:rank, keep] - dot(g_ref[:rank, :], z_all)) * scale
    packed[rows : rows + rank, :] = l_first
    for height in range(levels):
        shift = rank * height - rank * height // 128 * 128
        part = slice(height * rank, (height + 1) * rank)
        chain = jnp.concatenate([z_sib[height]] + z_own[height + 1 :], 0)
        row = got[height][1][:rank, :][:, shift:]
        l_part = (got[height][0][:rank, :] - dot(row, chain)) * scale
        l_out[part, keep] = l_part
        if height > 0:
            packed[rows + height * rank : rows + (height + 1) * rank, :] = l_part
    last.append(send(packed.at[areas[1]], other.at[areas[1]], 0, 3 * levels + 1))
    k_copy.wait_recv()
    packed[2 * rows : 2 * rows + rank, :] = k_ref[:rank, keep] * scale
    for height in range(levels):
        part = slice(height * rank, (height + 1) * rank)
        k_part = got[height][2][:rank, :] * scale
        k_out[part, keep] = k_part
        if height > 0:
            packed[2 * rows + height * rank : 2 * rows + (height + 1) * rank, :] = k_part
    last.append(send(packed.at[areas[2]], other.at[areas[2]], 0, 3 * levels + 2))
    for copy, target, area in zip(last, (z_out, l_out, k_out), areas):
        copy.wait_recv()
        target[:, give] = other[area, :]
    for copy in sends + last:
        copy.wait_send()


def tree_scratch(levels, rank, rows, cols, node_shape):
    half = cols // 2
    own, got = [], []
    for height in range(levels):
        left = rows - rank * height
        wide = rows - rank * height // 128 * 128
        group = [
            pltpu.VMEM((left, half), jnp.float32),
            pltpu.VMEM((left, wide), jnp.float32),
            pltpu.VMEM((left, half), jnp.float32),
        ]
        got += group
        if height > 0:
            own += group
    count = 4 * levels + 1
    return (
        [pltpu.VMEM((levels,) + node_shape, jnp.float32)]
        + own
        + got
        + [
            pltpu.VMEM((3 * rows, half), jnp.float32),
            pltpu.VMEM((3 * rows, half), jnp.float32),
            pltpu.SemaphoreType.DMA((levels,)),
            pltpu.SemaphoreType.DMA((count,)),
            pltpu.SemaphoreType.DMA((count,)),
        ]
    )


def tree(sums, weight_sums, gram, node_inverse, levels, rank, base):
    rows, cols = sums.shape
    vmem = pl.BlockSpec(memory_space=pltpu.VMEM)
    return pl.pallas_call(
        functools.partial(tree_kernel, levels, rank, base),
        out_shape=[jax.ShapeDtypeStruct((rows, cols), jnp.float32)] * 3,
        in_specs=[vmem] * 3 + [pl.BlockSpec(memory_space=pl.ANY)],
        out_specs=[vmem] * 3,
        scratch_shapes=tree_scratch(levels, rank, rows, cols, node_inverse.shape[1:]),
        compiler_params=pltpu.CompilerParams(collective_id=0, has_side_effects=True),
    )(sums, weight_sums, gram, node_inverse)


def whole_tree(leaf_rows, right_side, cotangent, basis, saved, node_inverse, levels, rank, tile):
    rows, depth = basis.shape
    cols = right_side.shape[1]
    vmem = pl.BlockSpec(memory_space=pltpu.VMEM)
    remote = pl.BlockSpec(memory_space=pl.ANY)
    return pl.pallas_call(
        functools.partial(whole_kernel, levels, rank, tile),
        out_shape=[jax.ShapeDtypeStruct((rows, cols), jnp.float32)] * 3,
        in_specs=[pl.BlockSpec(memory_space=pltpu.SMEM)] + [remote] * 5,
        out_specs=[vmem] * 3,
        scratch_shapes=[
            pltpu.VMEM((rows, cols), jnp.float32),
            pltpu.VMEM((rows, cols), jnp.float32),
            pltpu.VMEM((rows, rows), jnp.float32),
            pltpu.VMEM((depth, cols), jnp.float32),
            pltpu.VMEM((depth, cols), jnp.float32),
            pltpu.VMEM((rows, depth), jnp.float32),
            pltpu.VMEM((rows, depth), jnp.float32),
            pltpu.VMEM((rows, depth), jnp.bfloat16),
            pltpu.VMEM((rows, depth), jnp.bfloat16),
            pltpu.SemaphoreType.DMA((4, depth // tile)),
        ]
        + tree_scratch(levels, rank, rows, cols, node_inverse.shape[1:]),
        compiler_params=pltpu.CompilerParams(collective_id=0, has_side_effects=True),
    )(leaf_rows, right_side, cotangent, basis, saved, node_inverse)


def split(value):
    high = value.astype(jnp.bfloat16)
    return high, (value - high.astype(jnp.float32)).astype(jnp.bfloat16)


def triple(left, right, dims):
    def one(a, b):
        return lax.dot_general(a, b, (dims, ((), ())), preferred_element_type=jnp.float32)

    return one(left[0], right[1]) + one(left[1], right[0]) + one(left[0], right[0])


def lead_kernel(rows_ref, right_ref, cot_ref, basis_ref, saved_ref, s_ref, k_ref, g_ref):
    step = pl.program_id(0)
    tile = basis_ref.shape[1]
    place = step * tile + lax.broadcasted_iota(jnp.int32, (1, tile), 1)
    basis = split(jnp.where(place < rows_ref[0], basis_ref[...], 0.0))
    s_now = triple(basis, split(right_ref[...]), ((1,), (0,)))
    k_now = triple(basis, split(cot_ref[...]), ((1,), (0,)))
    g_now = triple(basis, split(saved_ref[...]), ((1,), (1,)))

    @pl.when(step == 0)
    def _():
        s_ref[...] = s_now
        k_ref[...] = k_now
        g_ref[...] = g_now

    @pl.when(step > 0)
    def _():
        s_ref[...] += s_now
        k_ref[...] += k_now
        g_ref[...] += g_now


def close_kernel(
    rows_ref, right_ref, cot_ref, saved_ref, z_ref, l_ref, k_ref, x_ref, left_ref, grad_ref
):
    tile = saved_ref.shape[1]
    first = pl.program_id(0) * tile
    down = first + lax.broadcasted_iota(jnp.int32, (tile, 1), 0)
    across = first + lax.broadcasted_iota(jnp.int32, (1, tile), 1)
    moved = triple(split(saved_ref[...]), split(z_ref[...]), ((0,), (0,)))
    solved = jnp.where(down < rows_ref[0], right_ref[...] - moved, 0.0)
    x_ref[...] = solved
    left = triple(split(l_ref[...]), split(cot_ref[...]), ((1,), (1,)))
    left_ref[...] = jnp.where(across < rows_ref[0], left, 0.0).astype(jnp.bfloat16)
    grad = triple(split(k_ref[...]), split(solved), ((1,), (1,)))
    grad_ref[...] = grad.astype(jnp.bfloat16)


def body(right_side, cotangent, coeff_basis, saved_basis, node_inverse, leaf_rows):
    row_count, cols = right_side.shape
    levels, rank = coeff_basis.shape[0], coeff_basis.shape[1]
    height = levels * rank
    base = lax.axis_size("leaf").bit_length() - 1 - levels
    basis = coeff_basis.reshape(height, row_count)
    saved = saved_basis.reshape(height, row_count)
    tile = math.gcd(row_count, TILE)
    grid = (row_count // tile,)
    count = pl.BlockSpec(memory_space=pltpu.SMEM)
    tall = pl.BlockSpec((tile, cols), lambda i: (i, 0))
    wide = pl.BlockSpec((height, tile), lambda i: (0, i))
    small = pl.BlockSpec((height, cols), lambda i: (0, 0))
    square = pl.BlockSpec((height, height), lambda i: (0, 0))
    if base == 0:
        z_own, l_sib, k_sib = whole_tree(
            leaf_rows, right_side, cotangent, basis, saved, node_inverse, levels, rank, tile
        )
    else:
        sums, weight_sums, gram = pl.pallas_call(
            lead_kernel,
            grid=grid,
            out_shape=[
                jax.ShapeDtypeStruct((height, cols), jnp.float32),
                jax.ShapeDtypeStruct((height, cols), jnp.float32),
                jax.ShapeDtypeStruct((height, height), jnp.float32),
            ],
            in_specs=[count, tall, tall, wide, wide],
            out_specs=[small, small, square],
        )(leaf_rows, right_side, cotangent, basis, saved)
        for bit in range(base):
            sums = sums + swapped(sums, bit)
            weight_sums = weight_sums + swapped(weight_sums, bit)
            gram = gram + swapped(gram, bit)
        z_own, l_sib, k_sib = tree(sums, weight_sums, gram, node_inverse, levels, rank, base)
    current, left, right = pl.pallas_call(
        close_kernel,
        grid=grid,
        out_shape=[
            jax.ShapeDtypeStruct((row_count, cols), jnp.float32),
            jax.ShapeDtypeStruct((height, row_count), jnp.bfloat16),
            jax.ShapeDtypeStruct((height, row_count), jnp.bfloat16),
        ],
        in_specs=[count, tall, tall, wide, small, small, small],
        out_specs=[tall, wide, wide],
    )(leaf_rows, right_side, cotangent, saved, z_own, l_sib, k_sib)
    shape = (levels, rank, row_count)
    return current, left.reshape(shape), right.reshape(shape)


def solution(mesh):
    in_specs = (
        P(("groups", "leaf"), None),
        P(("groups", "leaf"), None),
        P(None, None, ("groups", "leaf")),
        P(None, None, ("groups", "leaf")),
        P("groups", None, None),
        P(("groups", "leaf")),
    )
    out_specs = (
        P(("groups", "leaf"), None),
        P(None, None, ("groups", "leaf")),
        P(None, None, ("groups", "leaf")),
    )
    return jax.shard_map(body, mesh=mesh, in_specs=in_specs, out_specs=out_specs, check_vma=False)
```
